128 devices in a mesh: ctx: 16 (over z, y), exp: 8 (over x, core).
Axes of the slice: x: 4, y: 4, z: 4, core: 2. Of those that a mesh axis runs over, the one named last changes fastest.
Arguments:
- query_states: bfloat16 [8, 2048, 4096], P('exp', 'ctx'), may hold values from -95 to 95
- key_states: bfloat16 [8, 2048, 256], P('exp', 'ctx'), may hold values from -4.5 to 4.5
- value_states: bfloat16 [8, 2048, 256], P('exp', 'ctx'), may hold values from -57 to 57
- positions: int32 [8, 2048], P('exp'), may hold values from 0 to 2047, as said below
- lengths: int32 [8, 16], P('exp'), may hold values from 1 to 512, 2048 in all within a row
- routes: int32 [8, 2048, 8], P('exp', 'ctx'), may hold values from 0 to 127, as said below
- gate_weights: float32 [8, 2048, 8], P('exp', 'ctx'), may hold values from 0.05 to 0.3
- norm_gain: float32 [4096], replicated, may hold values from 0.1 to 1.9
- gate_proj: bfloat16 [128, 4096, 768], P(('ctx', 'exp')), may hold values from -0.09375 to 0.09375
- up_proj: bfloat16 [128, 4096, 768], P(('ctx', 'exp')), may hold values from -0.09375 to 0.09375
- down_proj: bfloat16 [128, 768, 4096], P(('ctx', 'exp')), may hold values from -0.21875 to 0.21875
Outputs:
- layer_out: bfloat16 [8, 2048, 4096], P('exp', 'ctx')
The draws below stay inside these ranges and needn't reach their ends.
Inputs may be any that keep to these rules, and one draw needn't show every extreme that they name: In each pack every position 0 to 2047 stands in one slot; the 128 slots of one device hold two runs of 64 consecutive positions. `routes`: each row names 8 different experts; at most 10 rows of one device name the same expert, and one expert is named by exactly 10 rows of every device.
All inputs are finite; a program needn't handle non-finite values.
Results may differ from the reference program's by a relative error of at most 0.011.
Values may be sent and summed in bfloat16 or wider, within the bound.
A program may use at most 128 MiB of HBM per device.

```python
import math
import jax
import jax.numpy as jnp
import numpy as np
from jax import lax

QH = 32
KVH = 2
HD = 128
D = 4096
HID = 768
EXPERTS = 128
TOP = 8
TOK_DEV = 128
PACKS = 8
SEQ = 2048
DOCS = 16
MEAN = 8
CAP = 10
N_CTX = 16
N_EXP = 8


def key_base(key):
    base_keys = jnp.clip(jax.random.normal(jax.random.fold_in(key, 101), (PACKS, SEQ, KVH, HD), jnp.float32), -4.5, 4.5)
    return base_keys


def draw_key_states(key, part):
    return key_base(key).reshape(PACKS, SEQ, KVH * HD).astype(jnp.bfloat16)


def draw_query_states(key, part):
    normal_part = jnp.clip(jax.random.normal(jax.random.fold_in(key, 202), (PACKS, SEQ, QH, HD), jnp.float32), -4.5, 4.5)
    return normal_part.reshape(PACKS, SEQ, QH * HD).astype(jnp.bfloat16)


def draw_value_states(key, part):
    normal_part = jnp.clip(jax.random.normal(jax.random.fold_in(key, 303), (PACKS, SEQ, KVH * HD), jnp.float32), -4.5, 4.5)
    columns = jnp.exp(jax.random.uniform(jax.random.fold_in(key, 304), (KVH * HD,), jnp.float32, math.log(0.3), math.log(3.0)))
    row_scale = jnp.exp(jax.random.uniform(jax.random.fold_in(key, 305), (PACKS, SEQ, 1), jnp.float32, math.log(0.3), math.log(3.0)))
    return (normal_part * columns * row_scale).astype(jnp.bfloat16)


def pack_order(pack_key):
    return jax.random.permutation(pack_key, 2 * SEQ // TOK_DEV)


def draw_positions(key, part):
    run_length = TOK_DEV // 2
    pack_keys = jax.random.split(jax.random.fold_in(key, 404), PACKS)
    orders = jax.vmap(pack_order)(pack_keys)
    slot_index = jnp.arange(SEQ)
    return (orders[:, slot_index // run_length] * run_length + slot_index % run_length).astype(jnp.int32)


def route_block(block_key, hot_expert):
    perm_key, score_key, column_key = jax.random.split(block_key, 3)
    expert_order = jax.random.permutation(perm_key, EXPERTS)
    row_index = jnp.arange(TOK_DEV)[:, None]
    column = jnp.arange(TOP)[None, :]
    cell_index = (row_index * TOP + column) % EXPERTS
    chosen = expert_order[cell_index]
    where_hot = jnp.sum(jnp.where(expert_order == hot_expert, jnp.arange(EXPERTS), 0))
    holds_hot = jnp.any(cell_index == where_hot, axis=1)
    scores = jax.random.randint(score_key, (TOK_DEV,), 0, 1 << 20) * TOK_DEV + jnp.arange(TOK_DEV)
    scores = jnp.where(holds_hot, -1, scores)
    extra_rows = CAP - MEAN
    picked = lax.top_k(scores, extra_rows)[1]
    marked = jnp.zeros((TOK_DEV,), jnp.int32).at[picked].set(1)
    target = jax.random.randint(column_key, (TOK_DEV, 1), 0, TOP)
    replace = (marked[:, None] == 1) & (column == target)
    return jnp.where(replace, hot_expert, chosen).astype(jnp.int32)


def draw_routes(key, part):
    hot_expert = jax.random.randint(jax.random.fold_in(key, 505), (), 0, EXPERTS)
    block_keys = jax.random.split(jax.random.fold_in(key, 506), PACKS * SEQ // TOK_DEV)
    blocks = jax.vmap(route_block, in_axes=(0, None))(block_keys, hot_expert)
    return blocks.reshape(PACKS, SEQ, TOP)


def levels(own_key, shape, shards, smallest, largest):
    gain, own = 1.0, jax.random.fold_in(own_key, 6)
    for dim, blocks in shards:
        heights = jnp.exp(jax.random.uniform(jax.random.fold_in(own, dim), (blocks,), jnp.float32, smallest / len(shards), largest / len(shards)))
        gain = gain * jnp.repeat(heights, shape[dim] // blocks).reshape([-1 if axis == dim else 1 for axis in range(len(shape))])
    return gain


def split_up(number_of, total, limit, lean):
    loads = [(1 << 20) // math.isqrt(rank ** lean) + 1 for rank in range(2, number_of + 1)]
    surplus, given = total - limit - (number_of - 1), [1] * (number_of - 1)
    while surplus > 0:
        candidates = [i for i in range(number_of - 1) if given[i] < limit]
        whole, budget = sum([loads[i] for i in candidates]), surplus
        for i in candidates:
            extra = min(limit - given[i], max(1, budget * loads[i] // whole), surplus)
            given[i] = given[i] + extra
            surplus = surplus - extra
    return np.array([limit] + given)


def ragged_sizes(own_key, number_of, total, limit, slope):
    if number_of == 2:
        one = jax.random.randint(own_key, (), max(1, total - limit), min(limit, total - 1) + 1)
        return jnp.stack([one, total - one])
    tallies = jnp.asarray(split_up(number_of, total, limit, slope), jnp.int32)
    twos = (number_of - 1) // 2
    source_of, receiver = tallies[1:1 + 2 * twos:2], tallies[2:2 + 2 * twos:2]
    room = jnp.minimum(source_of - 1, limit - receiver)
    shifted = jax.random.randint(jax.random.fold_in(own_key, 1), (twos,), 0, 1 << 20) % (room + 1)
    tallies = tallies.at[1:1 + 2 * twos:2].set(source_of - shifted).at[2:2 + 2 * twos:2].set(receiver + shifted)
    return tallies[jax.random.permutation(jax.random.fold_in(own_key, 2), number_of)]


def bell_draw(key, dims, scale, limit, shards=(), dtype=jnp.bfloat16):
    drawn = scale * jax.random.normal(key, dims, jnp.float32)
    if shards:
        drawn = drawn * levels(key, dims, shards, -0.22, 0.18)
    return jnp.clip(drawn, -limit, limit).astype(dtype)


def setup_inputs(seed: int = 0) -> dict:
    key_of = jax.random.split(jax.random.key(seed), 12)
    query_states = draw_query_states(jax.random.fold_in(key_of[11], 71), 0)
    key_states = draw_key_states(jax.random.fold_in(key_of[11], 71), 0)
    value_states = draw_value_states(jax.random.fold_in(key_of[11], 71), 0)
    positions = draw_positions(jax.random.fold_in(key_of[11], 71), 0)
    lengths = jax.vmap(lambda own: ragged_sizes(own, DOCS, SEQ, SEQ // 4, 2))(jax.random.split(key_of[4], PACKS)).reshape((PACKS, DOCS)).astype(jnp.int32)
    routes = draw_routes(jax.random.fold_in(key_of[11], 71), 0)
    gate_weights = jnp.clip(jnp.exp(math.log(0.3) - 1.7917595 * jax.random.uniform(key_of[6], (PACKS, SEQ, TOP), jnp.float32) ** levels(key_of[6], (PACKS, SEQ, TOP), ((0, 8), (1, 16)), -0.2, 0.2)), 0.05, 0.3)
    norm_gain = jnp.clip(1.0 + 0.18 * jax.random.normal(key_of[7], (D,), jnp.float32), 0.1, 1.9)
    gate_proj = bell_draw(key_of[8], (EXPERTS, D, HID), D ** -0.5, 0.09375, ((0, 128),))
    up_proj = bell_draw(key_of[9], (EXPERTS, D, HID), D ** -0.5, 0.09375, ((0, 128),))
    down_proj = bell_draw(key_of[10], (EXPERTS, HID, D), HID ** -0.5, 0.21875, ((0, 128),))
    return {"query_states": query_states, "key_states": key_states, "value_states": value_states, "positions": positions, "lengths": lengths, "routes": routes, "gate_weights": gate_weights, "norm_gain": norm_gain, "gate_proj": gate_proj, "up_proj": up_proj, "down_proj": down_proj}


neg_large = -1e+30
norm_eps = 1e-06

def doc_index(places, lengths):
    doc_ends = jnp.cumsum(lengths).astype(jnp.int32)
    return lax.optimization_barrier(jnp.sum((doc_ends[None, :] <= places[:, None]).astype(jnp.int32), axis=1))

def expert_apply(token_rows, gate_matrix, up_matrix, down_matrix):
    gate_act = jnp.dot(token_rows, gate_matrix, preferred_element_type=jnp.float32)
    up_act = jnp.dot(token_rows, up_matrix, preferred_element_type=jnp.float32)
    hidden = (jax.nn.silu(gate_act) * up_act).astype(jnp.bfloat16)
    return jnp.dot(hidden, down_matrix, preferred_element_type=jnp.float32).astype(jnp.bfloat16)

def attend_pack(packed):
    query_states, key_states, value_states, places, lengths = packed
    doc_ids = doc_index(places, lengths)
    visible = (doc_ids[None, :] == doc_ids[:, None]) & (places[None, :] <= places[:, None])
    per_group = QH // KVH
    query_groups = jnp.moveaxis(query_states.reshape(SEQ, KVH, per_group, HD), 1, 0).astype(jnp.float32)
    key_groups = jnp.moveaxis(key_states.reshape(SEQ, KVH, HD), 1, 0).astype(jnp.float32)
    value_groups = jnp.moveaxis(value_states.reshape(SEQ, KVH, HD), 1, 0).astype(jnp.float32)

    def attend_group(grouped):
        query_group, key_group, value_group = grouped
        scores = jnp.einsum('iqd,jd->qij', query_group, key_group, precision=lax.Precision.HIGHEST) * (1.0 / math.sqrt(HD))
        scores = jnp.where(visible[None], scores, neg_large)
        maxima = lax.optimization_barrier(jnp.max(scores, axis=2))
        exp_terms = jnp.where(visible[None], jnp.exp(scores - maxima[..., None]), 0.0)
        totals = lax.optimization_barrier(jnp.sum(exp_terms, axis=2))
        weights = lax.optimization_barrier(exp_terms.astype(jnp.bfloat16)).astype(jnp.float32)
        summed = jnp.einsum('qij,jd->iqd', weights, value_group, precision=lax.Precision.HIGHEST)
        return summed / jnp.transpose(totals)[..., None]
    head_outputs = lax.map(attend_group, (query_groups, key_groups, value_groups))
    return jnp.moveaxis(head_outputs, 0, 1).reshape(SEQ, QH * HD).astype(jnp.bfloat16)

def reference(query_states, key_states, value_states, positions, lengths, routes, gate_weights, norm_gain, gate_proj, up_proj, down_proj):
    attended = lax.map(attend_pack, (query_states, key_states, value_states, positions, lengths))
    widened = attended.astype(jnp.float32)
    normed = (widened * lax.rsqrt(lax.optimization_barrier(jnp.mean(widened * widened, axis=2, keepdims=True)) + norm_eps) * norm_gain).astype(jnp.bfloat16)
    flat_tokens = normed.reshape(PACKS * SEQ, D)
    flat_experts = routes.reshape(PACKS * SEQ * TOP).astype(jnp.int32)
    flat_gates = gate_weights.reshape(PACKS * SEQ * TOP)
    sort_order = jnp.argsort(flat_experts, stable=True).astype(jnp.int32)
    counts = jnp.bincount(flat_experts, length=EXPERTS).astype(jnp.int32)
    starts = (jnp.cumsum(counts) - counts).astype(jnp.int32)
    room_rows = N_CTX * N_EXP * CAP
    padded = jnp.concatenate([sort_order, jnp.zeros((room_rows,), jnp.int32)])

    def add_expert(accumulated, expert_id):
        slot_ids = lax.dynamic_slice_in_dim(padded, starts[expert_id].astype(jnp.int32), room_rows)
        is_live = jnp.arange(room_rows) < counts[expert_id]
        token_ids = slot_ids // TOP
        outputs = expert_apply(flat_tokens[token_ids], gate_proj[expert_id], up_proj[expert_id], down_proj[expert_id])
        scaled = jnp.where(is_live, flat_gates[slot_ids], 0.0)[:, None] * outputs.astype(jnp.float32)
        return (accumulated.at[token_ids].add(scaled), None)
    accumulated, ignored = lax.scan(add_expert, jnp.zeros((PACKS * SEQ, D), jnp.float32), jnp.arange(EXPERTS))
    mixed_out = widened.reshape(PACKS * SEQ, D) + accumulated
    return mixed_out.reshape(PACKS, SEQ, D).astype(jnp.bfloat16)
```

```python
import functools
import math

import jax
import jax.numpy as jnp
from jax import lax
from jax.experimental import pallas as pl
from jax.experimental.pallas import tpu as pltpu
from jax.sharding import PartitionSpec as P

QH = 32
HD = 128
D = 4096
HID = 768
TOK = 128
N_CTX = 16
N_EXP = 8
N_DEV = 128
SEQ = 2048
DOCS = 16
RUN = 64
BLOCKS = SEQ // RUN
WINDOW = 10
KEYS = WINDOW * RUN
QUARTER = D // 4
GROUP = 32
STRIDE = 37
MESH = pl.DeviceIdType.MESH

neg_large = -1e30
norm_eps = 1e-06


def peer(ctx, exp, delta):
    z, y, x, core = ctx // 4, ctx % 4, exp // 2, exp % 2
    dz, dy, dx, dcore = delta // 32, (delta // 8) % 4, (delta // 2) % 4, delta % 2
    return (
        ((z + dz) % 4) * 4 + (y + dy) % 4,
        ((x + dx) % 4) * 2 + (core + dcore) % 2,
    )


def gather_kernel(k_ref, v_ref, out_ref, send_sem, recv_sem, local_sem):
    ctx = lax.axis_index("ctx")
    exp = lax.axis_index("exp")
    barrier = pltpu.get_barrier_semaphore()
    peers = [lax.rem(ctx + step, N_CTX) for step in range(1, N_CTX)]
    for target in peers:
        pl.semaphore_signal(barrier, inc=1, device_id=(target, exp), device_id_type=MESH)
    pl.semaphore_wait(barrier, N_CTX - 1)
    copies = []
    for step, target in enumerate(peers):
        for which, source in enumerate((k_ref, v_ref)):
            copies.append(
                pltpu.make_async_remote_copy(
                    src_ref=source,
                    dst_ref=out_ref.at[ctx, which],
                    send_sem=send_sem.at[step, which],
                    recv_sem=recv_sem.at[step, which],
                    device_id=(target, exp),
                    device_id_type=MESH,
                )
            )
    for copy in copies:
        copy.start()
    own = [
        pltpu.make_async_copy(source, out_ref.at[ctx, which], local_sem.at[which])
        for which, source in enumerate((k_ref, v_ref))
    ]
    for copy in own:
        copy.start()
    for copy in copies:
        copy.wait()
    for copy in own:
        copy.wait()


def gather_keys(keys, values):
    return pl.pallas_call(
        gather_kernel,
        out_shape=jax.ShapeDtypeStruct((N_CTX, 2, TOK, 256), jnp.bfloat16),
        in_specs=[pl.BlockSpec(memory_space=pltpu.VMEM)] * 2,
        out_specs=pl.BlockSpec(memory_space=pltpu.VMEM),
        scratch_shapes=[
            pltpu.SemaphoreType.DMA((N_CTX - 1, 2)),
            pltpu.SemaphoreType.DMA((N_CTX - 1, 2)),
            pltpu.SemaphoreType.DMA((2,)),
        ],
        compiler_params=pltpu.CompilerParams(collective_id=0, has_side_effects=True),
        name="gather_keys",
    )(keys, values)


def attend_kernel(
    pos_ref, len_ref, q_ref, kv_ref, gain_ref, att_ref, norm_ref, where_ref, k_win, v_win
):
    ctx = lax.axis_index("ctx")
    for block in range(BLOCKS):
        where_ref[pos_ref[0, RUN * block] // RUN] = block
    ends = []
    total = jnp.int32(0)
    for doc in range(DOCS):
        total = total + len_ref[0, doc]
        ends.append(total)

    def one_run(run, carry):
        first_block = pos_ref[0, ctx * TOK + run * RUN] // RUN
        for step in range(WINDOW):
            block = where_ref[jnp.maximum(first_block - (WINDOW - 1) + step, 0)]
            rows = pl.ds(pl.multiple_of((block % 2) * RUN, RUN), RUN)
            k_win[pl.ds(step * RUN, RUN), :] = kv_ref[block // 2, 0, rows, :]
            v_win[pl.ds(step * RUN, RUN), :] = kv_ref[block // 2, 1, rows, :]
        own = first_block * RUN + lax.broadcasted_iota(jnp.int32, (RUN, 1), 0)
        start = jnp.zeros((RUN, 1), jnp.int32)
        for end in ends:
            start = jnp.maximum(start, jnp.where(own >= end, end, 0))
        places = (first_block - (WINDOW - 1)) * RUN + lax.broadcasted_iota(
            jnp.int32, (RUN, KEYS), 1
        )
        visible = (places >= start) & (places <= own)
        tokens = pl.ds(pl.multiple_of(run * RUN, RUN), RUN)

        def four_heads(part, inner):
            group = part // 4
            lanes = pl.ds(pl.multiple_of(group * HD, HD), HD)
            queries = jnp.concatenate(
                [
                    q_ref[tokens, pl.ds(pl.multiple_of((part * 4 + i) * HD, HD), HD)]
                    for i in range(4)
                ],
                axis=0,
            )
            scores = lax.dot_general(
                queries,
                k_win[:, lanes],
                (((1,), (1,)), ((), ())),
                preferred_element_type=jnp.float32,
            )
            scores = jnp.where(visible[None], scores.reshape(4, RUN, KEYS), neg_large)
            maxima = jnp.max(scores, axis=2, keepdims=True)
            probs = jnp.exp((scores - maxima) * (1.0 / math.sqrt(HD)))
            totals = jnp.sum(probs, axis=2, keepdims=True)
            summed = jnp.dot(
                probs.reshape(4 * RUN, KEYS).astype(jnp.bfloat16),
                v_win[:, lanes],
                preferred_element_type=jnp.float32,
            )
            result = (summed.reshape(4, RUN, HD) / totals).astype(jnp.bfloat16)
            for i in range(4):
                att_ref[tokens, pl.ds(pl.multiple_of((part * 4 + i) * HD, HD), HD)] = result[i]
            return inner

        lax.fori_loop(0, QH // 4, four_heads, 0)
        wide = att_ref[tokens, :].astype(jnp.float32)
        scale = lax.rsqrt(jnp.mean(wide * wide, axis=1, keepdims=True) + norm_eps)
        norm_ref[tokens, :] = (wide * scale * gain_ref[...]).astype(jnp.bfloat16)
        return carry

    lax.fori_loop(0, TOK // RUN, one_run, 0)


def attend(positions, lengths, queries, gathered, gain):
    return pl.pallas_call(
        attend_kernel,
        out_shape=[jax.ShapeDtypeStruct((TOK, D), jnp.bfloat16)] * 2,
        in_specs=[pl.BlockSpec(memory_space=pltpu.SMEM)] * 2
        + [pl.BlockSpec(memory_space=pltpu.VMEM)] * 3,
        out_specs=[pl.BlockSpec(memory_space=pltpu.VMEM)] * 2,
        scratch_shapes=[
            pltpu.SMEM((BLOCKS,), jnp.int32),
            pltpu.VMEM((KEYS, 256), jnp.bfloat16),
            pltpu.VMEM((KEYS, 256), jnp.bfloat16),
        ],
        name="attend",
    )(positions, lengths, queries, gathered, gain)


def slots_by_expert(routes_ref):
    experts = lax.broadcasted_iota(jnp.int32, (N_DEV, TOK), 0)
    named = jnp.zeros((N_DEV, TOK), jnp.float32)
    for k in range(8):
        named = named + (routes_ref[k : k + 1, :] == experts).astype(jnp.float32)
    earlier = (
        lax.broadcasted_iota(jnp.int32, (TOK, TOK), 0)
        < lax.broadcasted_iota(jnp.int32, (TOK, TOK), 1)
    ).astype(jnp.bfloat16)
    ranks = jnp.dot(named.astype(jnp.bfloat16), earlier, preferred_element_type=jnp.float32)
    return jnp.where(named > 0.5, ranks.astype(jnp.int32), -1)


def main_slots(slots):
    wide = jnp.broadcast_to(slots[:, None, :], (GROUP, 8, TOK))
    return (wide == lax.broadcasted_iota(jnp.int32, (GROUP, 8, TOK), 1)).reshape(GROUP * 8, TOK)


def extra_slots(slots, quarter):
    wide = jnp.broadcast_to(slots[:, None, :], (GROUP, 8, TOK))
    row = lax.broadcasted_iota(jnp.int32, (GROUP, 8, TOK), 1)
    hit = (wide == 8 + row % 2) & (row // 2 == quarter)
    return hit.reshape(GROUP * 8, TOK)


def pack_kernel(routes_ref, norm_ref, out_ref, slot_ref):
    step = pl.program_id(0)

    @pl.when(step == 0)
    def _():
        slot_ref[...] = slots_by_expert(routes_ref)

    slots = slot_ref[pl.ds(pl.multiple_of(step * GROUP, GROUP), GROUP), :]
    main = main_slots(slots).astype(jnp.float32).astype(jnp.bfloat16)
    extra = jnp.zeros((GROUP * 8, QUARTER), jnp.float32)
    for quarter in range(4):
        part = norm_ref[:, quarter * QUARTER : (quarter + 1) * QUARTER]
        rows = jnp.dot(main, part, preferred_element_type=jnp.float32)
        out_ref[:, quarter] = rows.astype(jnp.bfloat16).reshape(GROUP, 8, QUARTER)
        chosen = extra_slots(slots, quarter).astype(jnp.float32).astype(jnp.bfloat16)
        extra = extra + jnp.dot(chosen, part, preferred_element_type=jnp.float32)
    out_ref[:, 4] = extra.astype(jnp.bfloat16).reshape(GROUP, 8, QUARTER)


def pack(routes, normed):
    return pl.pallas_call(
        pack_kernel,
        grid=(N_DEV // GROUP,),
        out_shape=jax.ShapeDtypeStruct((N_DEV, 5, 8, QUARTER), jnp.bfloat16),
        in_specs=[
            pl.BlockSpec((8, TOK), lambda i: (0, 0)),
            pl.BlockSpec((TOK, D), lambda i: (0, 0)),
        ],
        out_specs=pl.BlockSpec((GROUP, 5, 8, QUARTER), lambda i: (i, 0, 0, 0)),
        scratch_shapes=[pltpu.VMEM((N_DEV, TOK), jnp.int32)],
        compiler_params=pltpu.CompilerParams(vmem_limit_bytes=40 << 20),
        name="pack_rows",
    )(routes, normed)


def exchange_kernel(in_ref, out_ref, send_sem, recv_sem, local_sem):
    ctx = lax.axis_index("ctx")
    exp = lax.axis_index("exp")
    me = ctx * N_EXP + exp
    barrier = pltpu.get_barrier_semaphore()

    def greet(delta, carry):
        pl.semaphore_signal(
            barrier, inc=1, device_id=peer(ctx, exp, delta), device_id_type=MESH
        )
        return carry

    lax.fori_loop(1, N_DEV, greet, 0)
    pl.semaphore_wait(barrier, N_DEV - 1)

    def message(i):
        delta = (i * STRIDE) % N_DEV
        target = peer(ctx, exp, delta)
        return pltpu.make_async_remote_copy(
            src_ref=in_ref.at[target[0] * N_EXP + target[1]],
            dst_ref=out_ref.at[me],
            send_sem=send_sem.at[delta],
            recv_sem=recv_sem.at[delta],
            device_id=target,
            device_id_type=MESH,
        )

    def send(i, carry):
        message(i).start()
        return carry

    def finish(i, carry):
        message(i).wait()
        return carry

    lax.fori_loop(1, N_DEV, send, 0)
    own = pltpu.make_async_copy(in_ref.at[me], out_ref.at[me], local_sem)
    own.start()
    lax.fori_loop(1, N_DEV, finish, 0)
    own.wait()


def exchange(messages, collective_id):
    return pl.pallas_call(
        exchange_kernel,
        out_shape=jax.ShapeDtypeStruct(messages.shape, messages.dtype),
        in_specs=[pl.BlockSpec(memory_space=pltpu.HBM)],
        out_specs=pl.BlockSpec(memory_space=pltpu.HBM),
        scratch_shapes=[
            pltpu.SemaphoreType.DMA((N_DEV,)),
            pltpu.SemaphoreType.DMA((N_DEV,)),
            pltpu.SemaphoreType.DMA,
        ],
        compiler_params=pltpu.CompilerParams(
            collective_id=collective_id, has_side_effects=True
        ),
        name="exchange_%d" % collective_id,
    )(messages)


def extra_pick(quarter):
    row = lax.broadcasted_iota(jnp.int32, (GROUP * 2, GROUP * 8), 0)
    column = lax.broadcasted_iota(jnp.int32, (GROUP * 2, GROUP * 8), 1)
    hit = column == (row // 2) * 8 + quarter * 2 + row % 2
    return hit.astype(jnp.float32).astype(jnp.bfloat16)


def expert_kernel(in_ref, gate_ref, up_ref, down_ref, out_ref):
    packed = in_ref[:, 4].reshape(GROUP * 8, QUARTER)
    gate = jnp.zeros((GROUP * 10, HID), jnp.float32)
    up = jnp.zeros((GROUP * 10, HID), jnp.float32)
    for quarter in range(4):
        extra = jnp.dot(extra_pick(quarter), packed, preferred_element_type=jnp.float32)
        rows = jnp.concatenate(
            [in_ref[:, quarter].reshape(GROUP * 8, QUARTER), extra.astype(jnp.bfloat16)], axis=0
        )
        span = slice(quarter * QUARTER, (quarter + 1) * QUARTER)
        gate = gate + jnp.dot(rows, gate_ref[span, :], preferred_element_type=jnp.float32)
        up = up + jnp.dot(rows, up_ref[span, :], preferred_element_type=jnp.float32)
    hidden = (gate / (1.0 + jnp.exp(-gate)) * up).astype(jnp.bfloat16)
    spread = jnp.zeros((GROUP * 8, QUARTER), jnp.float32)
    for quarter in range(4):
        span = slice(quarter * QUARTER, (quarter + 1) * QUARTER)
        result = jnp.dot(hidden, down_ref[:, span], preferred_element_type=jnp.float32)
        result = result.astype(jnp.bfloat16)
        out_ref[:, quarter] = result[: GROUP * 8].reshape(GROUP, 8, QUARTER)
        spread = spread + lax.dot_general(
            extra_pick(quarter),
            result[GROUP * 8 :],
            (((0,), (0,)), ((), ())),
            preferred_element_type=jnp.float32,
        )
    out_ref[:, 4] = spread.astype(jnp.bfloat16).reshape(GROUP, 8, QUARTER)


def expert(messages, gate, up, down):
    block = pl.BlockSpec((GROUP, 5, 8, QUARTER), lambda i: (i, 0, 0, 0))
    return pl.pallas_call(
        expert_kernel,
        grid=(N_DEV // GROUP,),
        out_shape=jax.ShapeDtypeStruct(messages.shape, messages.dtype),
        in_specs=[
            block,
            pl.BlockSpec((D, HID), lambda i: (0, 0), pipeline_mode=pl.Buffered(1)),
            pl.BlockSpec((D, HID), lambda i: (0, 0), pipeline_mode=pl.Buffered(1)),
            pl.BlockSpec((HID, D), lambda i: (0, 0), pipeline_mode=pl.Buffered(1)),
        ],
        out_specs=block,
        compiler_params=pltpu.CompilerParams(vmem_limit_bytes=56 << 20),
        name="expert",
    )(messages, gate, up, down)


def combine_kernel(routes_ref, gates_ref, att_ref, in_ref, out_ref, slot_ref, weight_ref, sum_ref):
    step = pl.program_id(0)

    @pl.when(step == 0)
    def _():
        slot_ref[...] = slots_by_expert(routes_ref)
        experts = lax.broadcasted_iota(jnp.int32, (N_DEV, TOK), 0)
        weight = jnp.zeros((N_DEV, TOK), jnp.float32)
        for k in range(8):
            weight = weight + jnp.where(
                routes_ref[k : k + 1, :] == experts, gates_ref[k : k + 1, :], 0.0
            )
        weight_ref[...] = weight
        sum_ref[...] = att_ref[...].astype(jnp.float32)

    span = pl.ds(pl.multiple_of(step * GROUP, GROUP), GROUP)
    slots = slot_ref[span, :]
    weights = jnp.broadcast_to(weight_ref[span, :][:, None, :], (GROUP, 8, TOK))
    weights = weights.reshape(GROUP * 8, TOK)

    def split(hit):
        value = jnp.where(hit, weights, 0.0)
        high = value.astype(jnp.bfloat16)
        low = (value - high.astype(jnp.float32)).astype(jnp.bfloat16)
        return jnp.concatenate([high, low], axis=1)

    def add_up(factors, rows):
        both = lax.dot_general(
            factors, rows, (((0,), (0,)), ((), ())), preferred_element_type=jnp.float32
        )
        return both[:TOK] + both[TOK:]

    main = split(main_slots(slots))
    packed = in_ref[:, 4].reshape(GROUP * 8, QUARTER)
    for quarter in range(4):
        part = slice(quarter * QUARTER, (quarter + 1) * QUARTER)
        rows = in_ref[:, quarter].reshape(GROUP * 8, QUARTER)
        sum_ref[:, part] += add_up(main, rows) + add_up(
            split(extra_slots(slots, quarter)), packed
        )

    @pl.when(step == pl.num_programs(0) - 1)
    def _():
        out_ref[...] = sum_ref[...].astype(jnp.bfloat16)


def combine(routes, gates, attended, messages):
    return pl.pallas_call(
        combine_kernel,
        grid=(N_DEV // GROUP,),
        out_shape=jax.ShapeDtypeStruct((TOK, D), jnp.bfloat16),
        in_specs=[
            pl.BlockSpec((8, TOK), lambda i: (0, 0)),
            pl.BlockSpec((8, TOK), lambda i: (0, 0)),
            pl.BlockSpec((TOK, D), lambda i: (0, 0)),
            pl.BlockSpec((GROUP, 5, 8, QUARTER), lambda i: (i, 0, 0, 0)),
        ],
        out_specs=pl.BlockSpec((TOK, D), lambda i: (0, 0)),
        scratch_shapes=[
            pltpu.VMEM((N_DEV, TOK), jnp.int32),
            pltpu.VMEM((N_DEV, TOK), jnp.float32),
            pltpu.VMEM((TOK, D), jnp.float32),
        ],
        compiler_params=pltpu.CompilerParams(vmem_limit_bytes=40 << 20),
        name="combine",
    )(routes, gates, attended, messages)


def local(
    query_states,
    key_states,
    value_states,
    positions,
    lengths,
    routes,
    gate_weights,
    norm_gain,
    gate_proj,
    up_proj,
    down_proj,
):
    gathered = gather_keys(key_states[0], value_states[0])
    attended, normed = attend(
        positions, lengths, query_states[0], gathered, norm_gain.reshape(1, D)
    )
    by_rank = routes[0].T
    outgoing = pack(by_rank, normed)
    arrived = exchange(outgoing, 1)
    results = expert(arrived, gate_proj[0], up_proj[0], down_proj[0])
    returned = exchange(results, 2)
    return combine(by_rank, gate_weights[0].T, attended, returned)[None]


def solution(mesh):
    in_specs = (
        P("exp", "ctx", None),
        P("exp", "ctx", None),
        P("exp", "ctx", None),
        P("exp", None),
        P("exp", None),
        P("exp", "ctx", None),
        P("exp", "ctx", None),
        P(),
        P(("ctx", "exp"), None, None),
        P(("ctx", "exp"), None, None),
        P(("ctx", "exp"), None, None),
    )
    out_specs = P("exp", "ctx", None)
    return jax.shard_map(local, mesh=mesh, in_specs=in_specs, out_specs=out_specs, check_vma=False)
```

```python
import functools
import math

import jax
import jax.numpy as jnp
from jax import lax
from jax.experimental import pallas as pl
from jax.experimental.pallas import tpu as pltpu
from jax.sharding import PartitionSpec as P

QH = 32
HD = 128
D = 4096
HID = 768
TOK = 128
N_CTX = 16
N_EXP = 8
N_DEV = 128
SEQ = 2048
DOCS = 16
RUN = 64
BLOCKS = SEQ // RUN
WINDOW = 10
KEYS = WINDOW * RUN
QUARTER = D // 4
GROUP = 32
PARTS = N_DEV // GROUP
STRIDE = 91
MESH = pl.DeviceIdType.MESH

neg_large = -1e30
norm_eps = 1e-06


def peer(ctx, exp, delta):
    z, y, x, core = ctx // 4, ctx % 4, exp // 2, exp % 2
    dz, dy, dx, dcore = delta // 32, (delta // 8) % 4, (delta // 2) % 4, delta % 2
    return (
        ((z + dz) % 4) * 4 + (y + dy) % 4,
        ((x + dx) % 4) * 2 + (core + dcore) % 2,
    )


def gather_kernel(k_ref, v_ref, out_ref, send_sem, recv_sem, local_sem):
    ctx = lax.axis_index("ctx")
    exp = lax.axis_index("exp")

    def along(axis, origin, step):
        oz, oy = origin // 4, origin % 4
        if axis == 0:
            return oz * 4 + (oy + step) % 4
        return ((oz + step) % 4) * 4 + oy

    barrier = pltpu.get_barrier_semaphore()
    for axis in range(2):
        for step in range(1, 4):
            pl.semaphore_signal(
                barrier, inc=1, device_id=(along(axis, ctx, step), exp), device_id_type=MESH
            )
    pl.semaphore_wait(barrier, 6)

    started = []
    for which in range(2):
        for step in range(1, 4):
            sent = pltpu.make_async_remote_copy(
                src_ref=(k_ref, v_ref)[which],
                dst_ref=out_ref.at[ctx, which],
                send_sem=send_sem.at[which, 0, step],
                recv_sem=recv_sem.at[which, 0, step],
                device_id=(along(which, ctx, step), exp),
                device_id_type=MESH,
            )
            sent.start()
            started.append(sent)

    def pass_on(which, first):
        origin = along(which, ctx, 4 - first) if first else ctx
        for step in range(1, 4):
            sent = pltpu.make_async_remote_copy(
                src_ref=out_ref.at[origin, which] if first else (k_ref, v_ref)[which],
                dst_ref=out_ref.at[origin, which],
                send_sem=send_sem.at[which, 1 + first, step],
                recv_sem=recv_sem.at[which, 1 + first, step],
                device_id=(along(1 - which, ctx, step), exp),
                device_id_type=MESH,
            )
            sent.start()
            started.append(sent)

    for which in range(2):
        pass_on(which, 0)
    own = [
        pltpu.make_async_copy(source, out_ref.at[ctx, which], local_sem.at[which])
        for which, source in enumerate((k_ref, v_ref))
    ]
    for sent in own:
        sent.start()
    for first in (1, 3, 2):
        for which in range(2):
            started[which * 3 + first - 1].wait_recv()
            pass_on(which, first)
    for index, sent in enumerate(started):
        sent.wait_send()
        if index >= 6:
            sent.wait_recv()
    for sent in own:
        sent.wait()


def gather_keys(keys, values):
    return pl.pallas_call(
        gather_kernel,
        out_shape=jax.ShapeDtypeStruct((N_CTX, 2, TOK, 256), jnp.bfloat16),
        in_specs=[pl.BlockSpec(memory_space=pltpu.VMEM)] * 2,
        out_specs=pl.BlockSpec(memory_space=pltpu.VMEM),
        scratch_shapes=[
            pltpu.SemaphoreType.DMA((2, 5, 4)),
            pltpu.SemaphoreType.DMA((2, 5, 4)),
            pltpu.SemaphoreType.DMA((2,)),
        ],
        compiler_params=pltpu.CompilerParams(collective_id=0, has_side_effects=True),
        name="gather_keys",
    )(keys, values)


def attend_kernel(
    pos_ref, len_ref, q_ref, kv_ref, gain_ref, att_ref, norm_ref, where_ref, k_win, v_win
):
    ctx = lax.axis_index("ctx")
    for block in range(BLOCKS):
        where_ref[pos_ref[0, RUN * block] // RUN] = block
    ends = []
    total = jnp.int32(0)
    for doc in range(DOCS):
        total = total + len_ref[0, doc]
        ends.append(total)

    def one_run(run, carry):
        first_block = pos_ref[0, ctx * TOK + run * RUN] // RUN
        for step in range(WINDOW):
            block = where_ref[jnp.maximum(first_block - (WINDOW - 1) + step, 0)]
            rows = pl.ds(pl.multiple_of((block % 2) * RUN, RUN), RUN)
            k_win[pl.ds(step * RUN, RUN), :] = kv_ref[block // 2, 0, rows, :]
            v_win[pl.ds(step * RUN, RUN), :] = kv_ref[block // 2, 1, rows, :]
        own = first_block * RUN + lax.broadcasted_iota(jnp.int32, (RUN, 1), 0)
        start = jnp.zeros((RUN, 1), jnp.int32)
        for end in ends:
            start = jnp.maximum(start, jnp.where(own >= end, end, 0))
        places = (first_block - (WINDOW - 1)) * RUN + lax.broadcasted_iota(
            jnp.int32, (RUN, KEYS), 1
        )
        visible = (places >= start) & (places <= own)
        tokens = pl.ds(pl.multiple_of(run * RUN, RUN), RUN)

        def four_heads(part, inner):
            group = part // 4
            lanes = pl.ds(pl.multiple_of(group * HD, HD), HD)
            queries = jnp.concatenate(
                [
                    q_ref[tokens, pl.ds(pl.multiple_of((part * 4 + i) * HD, HD), HD)]
                    for i in range(4)
                ],
                axis=0,
            )
            scores = lax.dot_general(
                queries,
                k_win[:, lanes],
                (((1,), (1,)), ((), ())),
                preferred_element_type=jnp.float32,
            )
            scores = jnp.where(visible[None], scores.reshape(4, RUN, KEYS), neg_large)
            maxima = jnp.max(scores, axis=2, keepdims=True)
            probs = jnp.exp((scores - maxima) * (1.0 / math.sqrt(HD)))
            totals = jnp.sum(probs, axis=2, keepdims=True)
            summed = jnp.dot(
                probs.reshape(4 * RUN, KEYS).astype(jnp.bfloat16),
                v_win[:, lanes],
                preferred_element_type=jnp.float32,
            )
            result = (summed.reshape(4, RUN, HD) / totals).astype(jnp.bfloat16)
            for i in range(4):
                att_ref[tokens, pl.ds(pl.multiple_of((part * 4 + i) * HD, HD), HD)] = result[i]
            return inner

        lax.fori_loop(0, QH // 4, four_heads, 0)
        wide = att_ref[tokens, :].astype(jnp.float32)
        scale = lax.rsqrt(jnp.mean(wide * wide, axis=1, keepdims=True) + norm_eps)
        norm_ref[tokens, :] = (wide * scale * gain_ref[...]).astype(jnp.bfloat16)
        return carry

    lax.fori_loop(0, TOK // RUN, one_run, 0)


def attend(positions, lengths, queries, gathered, gain):
    return pl.pallas_call(
        attend_kernel,
        out_shape=[jax.ShapeDtypeStruct((TOK, D), jnp.bfloat16)] * 2,
        in_specs=[pl.BlockSpec(memory_space=pltpu.SMEM)] * 2
        + [pl.BlockSpec(memory_space=pltpu.VMEM)] * 3,
        out_specs=[pl.BlockSpec(memory_space=pltpu.VMEM)] * 2,
        scratch_shapes=[
            pltpu.SMEM((BLOCKS,), jnp.int32),
            pltpu.VMEM((KEYS, 256), jnp.bfloat16),
            pltpu.VMEM((KEYS, 256), jnp.bfloat16),
        ],
        name="attend",
    )(positions, lengths, queries, gathered, gain)


def slots_by_expert(routes_ref):
    experts = lax.broadcasted_iota(jnp.int32, (N_DEV, TOK), 0)
    named = jnp.zeros((N_DEV, TOK), jnp.float32)
    for k in range(8):
        named = named + (routes_ref[k : k + 1, :] == experts).astype(jnp.float32)
    earlier = (
        lax.broadcasted_iota(jnp.int32, (TOK, TOK), 0)
        < lax.broadcasted_iota(jnp.int32, (TOK, TOK), 1)
    ).astype(jnp.bfloat16)
    ranks = jnp.dot(named.astype(jnp.bfloat16), earlier, preferred_element_type=jnp.float32)
    return jnp.where(named > 0.5, ranks.astype(jnp.int32), -1)


def main_slots(slots):
    wide = jnp.broadcast_to(slots[:, None, :], (GROUP, 8, TOK))
    return (wide == lax.broadcasted_iota(jnp.int32, (GROUP, 8, TOK), 1)).reshape(GROUP * 8, TOK)


def extra_slots(slots, quarter):
    wide = jnp.broadcast_to(slots[:, None, :], (GROUP, 8, TOK))
    row = lax.broadcasted_iota(jnp.int32, (GROUP, 8, TOK), 1)
    hit = (wide == 8 + row % 2) & (row // 2 == quarter)
    return hit.reshape(GROUP * 8, TOK)


def extra_pick(quarter):
    row = lax.broadcasted_iota(jnp.int32, (GROUP * 2, GROUP * 8), 0)
    column = lax.broadcasted_iota(jnp.int32, (GROUP * 2, GROUP * 8), 1)
    hit = column == (row // 2) * 8 + quarter * 2 + row % 2
    return hit.astype(jnp.float32).astype(jnp.bfloat16)


def spans(quarter):
    return slice(quarter * QUARTER, (quarter + 1) * QUARTER)


def moe_kernel(
    routes_ref,
    gates_ref,
    att_ref,
    norm_ref,
    gate_hbm,
    up_hbm,
    down_hbm,
    out_ref,
    arrived,
    returned,
    gate_ref,
    up_ref,
    down_ref,
    messages,
    stage,
    slot_ref,
    weight_ref,
    slot_part,
    weight_part,
    sum_ref,
    send_out,
    recv_out,
    send_back,
    recv_back,
    local_sem,
):
    ctx = lax.axis_index("ctx")
    exp = lax.axis_index("exp")

    loads = [
        pltpu.make_async_copy(source, target, local_sem.at[i])
        for i, (source, target) in enumerate(
            ((gate_hbm, gate_ref), (up_hbm, up_ref), (down_hbm, down_ref))
        )
    ]
    for load in loads:
        load.start()

    barrier = pltpu.get_barrier_semaphore()

    def greet(delta, carry):
        pl.semaphore_signal(
            barrier, inc=1, device_id=peer(ctx, exp, delta), device_id_type=MESH
        )
        return carry

    lax.fori_loop(1, N_DEV, greet, 0)

    slot_ref[...] = slots_by_expert(routes_ref)
    experts = lax.broadcasted_iota(jnp.int32, (N_DEV, TOK), 0)
    weight = jnp.zeros((N_DEV, TOK), jnp.float32)
    for k in range(8):
        weight = weight + jnp.where(
            routes_ref[k : k + 1, :] == experts, gates_ref[k : k + 1, :], 0.0
        )
    weight_ref[...] = weight
    sum_ref[...] = att_ref[...].astype(jnp.float32)

    def outward(i):
        delta = (i * STRIDE) % N_DEV
        return pltpu.make_async_remote_copy(
            src_ref=messages.at[i],
            dst_ref=arrived.at[i],
            send_sem=send_out.at[i],
            recv_sem=recv_out.at[i],
            device_id=peer(ctx, exp, delta),
            device_id_type=MESH,
        )

    def homeward(i):
        delta = (i * STRIDE) % N_DEV
        dz, dy, dx, dcore = delta // 32, (delta // 8) % 4, (delta // 2) % 4, delta % 2
        back = ((4 - dz) % 4) * 32 + ((4 - dy) % 4) * 8 + ((4 - dx) % 4) * 2 + dcore
        return pltpu.make_async_remote_copy(
            src_ref=messages.at[i],
            dst_ref=returned.at[i],
            send_sem=send_back.at[i],
            recv_sem=recv_back.at[i],
            device_id=peer(ctx, exp, back),
            device_id_type=MESH,
        )

    own_out = pltpu.make_async_copy(messages.at[0], arrived.at[0], local_sem.at[3])
    own_back = pltpu.make_async_copy(messages.at[0], returned.at[0], local_sem.at[4])

    def each(part, remote, own):
        def one(j, carry):
            i = part * GROUP + j

            @pl.when(i > 0)
            def _():
                remote(i)

            @pl.when(i == 0)
            def _():
                own()

            return carry

        lax.fori_loop(0, GROUP, one, 0)

    def pick_rows(part):
        def one(j, carry):
            target = peer(ctx, exp, ((part * GROUP + j) * STRIDE) % N_DEV)
            row = target[0] * N_EXP + target[1]
            slot_part[pl.ds(j, 1), :] = slot_ref[pl.ds(row, 1), :]
            weight_part[pl.ds(j, 1), :] = weight_ref[pl.ds(row, 1), :]
            return carry

        lax.fori_loop(0, GROUP, one, 0)
        return slot_part[...]

    def pack_part(part, carry):
        slots = pick_rows(part)
        span = pl.ds(part * GROUP, GROUP)
        main = main_slots(slots).astype(jnp.float32).astype(jnp.bfloat16)
        extra = jnp.zeros((GROUP * 8, QUARTER), jnp.float32)
        for quarter in range(4):
            normed = norm_ref[:, spans(quarter)]
            rows = jnp.dot(main, normed, preferred_element_type=jnp.float32)
            messages[span, quarter] = rows.astype(jnp.bfloat16).reshape(GROUP, 8, QUARTER)
            chosen = extra_slots(slots, quarter).astype(jnp.float32).astype(jnp.bfloat16)
            extra = extra + jnp.dot(chosen, normed, preferred_element_type=jnp.float32)
        messages[span, 4] = extra.astype(jnp.bfloat16).reshape(GROUP, 8, QUARTER)

        @pl.when(part == 0)
        def _():
            pl.semaphore_wait(barrier, N_DEV - 1)

        each(part, lambda i: outward(i).start(), own_out.start)
        return carry

    lax.fori_loop(0, PARTS, pack_part, 0)
    for load in loads:
        load.wait()

    def fetch(source, part):
        copy = pltpu.make_async_copy(
            source.at[pl.ds(part * GROUP, GROUP)], stage, local_sem.at[5]
        )
        copy.start()
        copy.wait()

    def expert_part(part, carry):
        each(part, lambda i: outward(i).wait(), own_out.wait)
        fetch(arrived, part)
        span = pl.ds(part * GROUP, GROUP)
        packed = stage[:, 4].reshape(GROUP * 8, QUARTER)
        gate = jnp.zeros((GROUP * 10, HID), jnp.float32)
        up = jnp.zeros((GROUP * 10, HID), jnp.float32)
        for quarter in range(4):
            extra = jnp.dot(extra_pick(quarter), packed, preferred_element_type=jnp.float32)
            rows = jnp.concatenate(
                [stage[:, quarter].reshape(GROUP * 8, QUARTER), extra.astype(jnp.bfloat16)],
                axis=0,
            )
            gate = gate + jnp.dot(
                rows, gate_ref[spans(quarter), :], preferred_element_type=jnp.float32
            )
            up = up + jnp.dot(
                rows, up_ref[spans(quarter), :], preferred_element_type=jnp.float32
            )
        hidden = (gate / (1.0 + jnp.exp(-gate)) * up).astype(jnp.bfloat16)
        spread = jnp.zeros((GROUP * 8, QUARTER), jnp.float32)
        for quarter in range(4):
            result = jnp.dot(
                hidden, down_ref[:, spans(quarter)], preferred_element_type=jnp.float32
            ).astype(jnp.bfloat16)
            messages[span, quarter] = result[: GROUP * 8].reshape(GROUP, 8, QUARTER)
            spread = spread + lax.dot_general(
                extra_pick(quarter),
                result[GROUP * 8 :],
                (((0,), (0,)), ((), ())),
                preferred_element_type=jnp.float32,
            )
        messages[span, 4] = spread.astype(jnp.bfloat16).reshape(GROUP, 8, QUARTER)
        each(part, lambda i: homeward(i).start(), own_back.start)
        return carry

    lax.fori_loop(0, PARTS, expert_part, 0)

    def add_up(factors, rows):
        both = lax.dot_general(
            factors, rows, (((0,), (0,)), ((), ())), preferred_element_type=jnp.float32
        )
        return both[:TOK] + both[TOK:]

    def combine_part(part, carry):
        slots = pick_rows(part)
        weights = jnp.broadcast_to(weight_part[...][:, None, :], (GROUP, 8, TOK))
        weights = weights.reshape(GROUP * 8, TOK)

        def split(hit):
            value = jnp.where(hit, weights, 0.0)
            high = value.astype(jnp.bfloat16)
            low = (value - high.astype(jnp.float32)).astype(jnp.bfloat16)
            return jnp.concatenate([high, low], axis=1)

        each(part, lambda i: homeward(i).wait(), own_back.wait)
        fetch(returned, part)
        main = split(main_slots(slots))
        packed = stage[:, 4].reshape(GROUP * 8, QUARTER)
        for quarter in range(4):
            rows = stage[:, quarter].reshape(GROUP * 8, QUARTER)
            sum_ref[:, spans(quarter)] += add_up(main, rows) + add_up(
                split(extra_slots(slots, quarter)), packed
            )
        return carry

    lax.fori_loop(0, PARTS, combine_part, 0)
    out_ref[...] = sum_ref[...].astype(jnp.bfloat16)


def moe(routes, gates, attended, normed, gate, up, down):
    wire = (N_DEV, 5, 8, QUARTER)
    vmem = pl.BlockSpec(memory_space=pltpu.VMEM)
    hbm = pl.BlockSpec(memory_space=pltpu.HBM)
    return pl.pallas_call(
        moe_kernel,
        out_shape=[
            jax.ShapeDtypeStruct((TOK, D), jnp.bfloat16),
            jax.ShapeDtypeStruct(wire, jnp.bfloat16),
            jax.ShapeDtypeStruct(wire, jnp.bfloat16),
        ],
        in_specs=[vmem] * 4 + [hbm] * 3,
        out_specs=[vmem, hbm, hbm],
        scratch_shapes=[
            pltpu.VMEM((D, HID), jnp.bfloat16),
            pltpu.VMEM((D, HID), jnp.bfloat16),
            pltpu.VMEM((HID, D), jnp.bfloat16),
            pltpu.VMEM(wire, jnp.bfloat16),
            pltpu.VMEM((GROUP, 5, 8, QUARTER), jnp.bfloat16),
            pltpu.VMEM((N_DEV, TOK), jnp.int32),
            pltpu.VMEM((N_DEV, TOK), jnp.float32),
            pltpu.VMEM((GROUP, TOK), jnp.int32),
            pltpu.VMEM((GROUP, TOK), jnp.float32),
            pltpu.VMEM((TOK, D), jnp.float32),
            pltpu.SemaphoreType.DMA((N_DEV,)),
            pltpu.SemaphoreType.DMA((N_DEV,)),
            pltpu.SemaphoreType.DMA((N_DEV,)),
            pltpu.SemaphoreType.DMA((N_DEV,)),
            pltpu.SemaphoreType.DMA((6,)),
        ],
        compiler_params=pltpu.CompilerParams(
            collective_id=1, has_side_effects=True, vmem_limit_bytes=58 << 20
        ),
        name="moe",
    )(routes, gates, attended, normed, gate, up, down)[0]


def local(
    query_states,
    key_states,
    value_states,
    positions,
    lengths,
    routes,
    gate_weights,
    norm_gain,
    gate_proj,
    up_proj,
    down_proj,
):
    gathered = gather_keys(key_states[0], value_states[0])
    attended, normed = attend(
        positions, lengths, query_states[0], gathered, norm_gain.reshape(1, D)
    )
    out = moe(
        routes[0].T,
        gate_weights[0].T,
        attended,
        normed,
        gate_proj[0],
        up_proj[0],
        down_proj[0],
    )
    return out[None]


def solution(mesh):
    in_specs = (
        P("exp", "ctx", None),
        P("exp", "ctx", None),
        P("exp", "ctx", None),
        P("exp", None),
        P("exp", None),
        P("exp", "ctx", None),
        P("exp", "ctx", None),
        P(),
        P(("ctx", "exp"), None, None),
        P(("ctx", "exp"), None, None),
        P(("ctx", "exp"), None, None),
    )
    out_specs = P("exp", "ctx", None)
    return jax.shard_map(local, mesh=mesh, in_specs=in_specs, out_specs=out_specs, check_vma=False)
```

```python
import functools
import math

import jax
import jax.numpy as jnp
from jax import lax
from jax.experimental import pallas as pl
from jax.experimental.pallas import tpu as pltpu
from jax.sharding import PartitionSpec as P

QH = 32
HD = 128
D = 4096
HID = 768
TOK = 128
N_CTX = 16
N_DEV = 128
SEQ = 2048
DOCS = 16
RUN = 64
BLOCKS = SEQ // RUN
WINDOW = 10
KEYS = WINDOW * RUN
MESH = pl.DeviceIdType.MESH

neg_large = -1e30
norm_eps = 1e-06


def gather_kernel(k_ref, v_ref, out_ref, send_sem, recv_sem, local_sem):
    ctx = lax.axis_index("ctx")
    exp = lax.axis_index("exp")

    def along(axis, origin, step):
        oz, oy = origin // 4, origin % 4
        if axis == 0:
            return oz * 4 + (oy + step) % 4
        return ((oz + step) % 4) * 4 + oy

    barrier = pltpu.get_barrier_semaphore()
    for axis in range(2):
        for step in range(1, 4):
            pl.semaphore_signal(
                barrier, inc=1, device_id=(along(axis, ctx, step), exp), device_id_type=MESH
            )
    pl.semaphore_wait(barrier, 6)

    started = []
    for which in range(2):
        for step in range(1, 4):
            sent = pltpu.make_async_remote_copy(
                src_ref=(k_ref, v_ref)[which],
                dst_ref=out_ref.at[ctx, which],
                send_sem=send_sem.at[which, 0, step],
                recv_sem=recv_sem.at[which, 0, step],
                device_id=(along(which, ctx, step), exp),
                device_id_type=MESH,
            )
            sent.start()
            started.append(sent)

    def pass_on(which, first):
        origin = along(which, ctx, 4 - first) if first else ctx
        for step in range(1, 4):
            sent = pltpu.make_async_remote_copy(
                src_ref=out_ref.at[origin, which] if first else (k_ref, v_ref)[which],
                dst_ref=out_ref.at[origin, which],
                send_sem=send_sem.at[which, 1 + first, step],
                recv_sem=recv_sem.at[which, 1 + first, step],
                device_id=(along(1 - which, ctx, step), exp),
                device_id_type=MESH,
            )
            sent.start()
            started.append(sent)

    for which in range(2):
        pass_on(which, 0)
    own = [
        pltpu.make_async_copy(source, out_ref.at[ctx, which], local_sem.at[which])
        for which, source in enumerate((k_ref, v_ref))
    ]
    for sent in own:
        sent.start()
    for first in (1, 3, 2):
        for which in range(2):
            started[which * 3 + first - 1].wait_recv()
            pass_on(which, first)
    for index, sent in enumerate(started):
        sent.wait_send()
        if index >= 6:
            sent.wait_recv()
    for sent in own:
        sent.wait()


def gather_keys(keys, values):
    return pl.pallas_call(
        gather_kernel,
        out_shape=jax.ShapeDtypeStruct((N_CTX, 2, TOK, 256), jnp.bfloat16),
        in_specs=[pl.BlockSpec(memory_space=pltpu.VMEM)] * 2,
        out_specs=pl.BlockSpec(memory_space=pltpu.VMEM),
        scratch_shapes=[
            pltpu.SemaphoreType.DMA((2, 5, 4)),
            pltpu.SemaphoreType.DMA((2, 5, 4)),
            pltpu.SemaphoreType.DMA((2,)),
        ],
        compiler_params=pltpu.CompilerParams(collective_id=0, has_side_effects=True),
        name="gather_keys",
    )(keys, values)


def attend_kernel(
    pos_ref, len_ref, q_ref, kv_ref, gain_ref, att_ref, norm_ref, where_ref, k_win, v_win
):
    ctx = lax.axis_index("ctx")
    for block in range(BLOCKS):
        where_ref[pos_ref[0, RUN * block] // RUN] = block
    ends = []
    total = jnp.int32(0)
    for doc in range(DOCS):
        total = total + len_ref[0, doc]
        ends.append(total)

    def one_run(run, carry):
        first_block = pos_ref[0, ctx * TOK + run * RUN] // RUN
        for step in range(WINDOW):
            block = where_ref[jnp.maximum(first_block - (WINDOW - 1) + step, 0)]
            rows = pl.ds(pl.multiple_of((block % 2) * RUN, RUN), RUN)
            k_win[pl.ds(step * RUN, RUN), :] = kv_ref[block // 2, 0, rows, :]
            v_win[pl.ds(step * RUN, RUN), :] = kv_ref[block // 2, 1, rows, :]
        own = first_block * RUN + lax.broadcasted_iota(jnp.int32, (RUN, 1), 0)
        start = jnp.zeros((RUN, 1), jnp.int32)
        for end in ends:
            start = jnp.maximum(start, jnp.where(own >= end, end, 0))
        places = (first_block - (WINDOW - 1)) * RUN + lax.broadcasted_iota(
            jnp.int32, (RUN, KEYS), 1
        )
        visible = (places >= start) & (places <= own)
        tokens = pl.ds(pl.multiple_of(run * RUN, RUN), RUN)

        def four_heads(part, inner):
            group = part // 4
            lanes = pl.ds(pl.multiple_of(group * HD, HD), HD)
            queries = jnp.concatenate(
                [
                    q_ref[tokens, pl.ds(pl.multiple_of((part * 4 + i) * HD, HD), HD)]
                    for i in range(4)
                ],
                axis=0,
            )
            scores = lax.dot_general(
                queries,
                k_win[:, lanes],
                (((1,), (1,)), ((), ())),
                preferred_element_type=jnp.float32,
            )
            scores = jnp.where(visible[None], scores.reshape(4, RUN, KEYS), neg_large)
            maxima = jnp.max(scores, axis=2, keepdims=True)
            probs = jnp.exp((scores - maxima) * (1.0 / math.sqrt(HD)))
            totals = jnp.sum(probs, axis=2, keepdims=True)
            summed = jnp.dot(
                probs.reshape(4 * RUN, KEYS).astype(jnp.bfloat16),
                v_win[:, lanes],
                preferred_element_type=jnp.float32,
            )
            result = (summed.reshape(4, RUN, HD) / totals).astype(jnp.bfloat16)
            for i in range(4):
                att_ref[tokens, pl.ds(pl.multiple_of((part * 4 + i) * HD, HD), HD)] = result[i]
            return inner

        lax.fori_loop(0, QH // 4, four_heads, 0)
        wide = att_ref[tokens, :].astype(jnp.float32)
        scale = lax.rsqrt(jnp.mean(wide * wide, axis=1, keepdims=True) + norm_eps)
        norm_ref[tokens, :] = (wide * scale * gain_ref[...]).astype(jnp.bfloat16)
        return carry

    lax.fori_loop(0, TOK // RUN, one_run, 0)


def attend(positions, lengths, queries, gathered, gain):
    return pl.pallas_call(
        attend_kernel,
        out_shape=[jax.ShapeDtypeStruct((TOK, D), jnp.bfloat16)] * 2,
        in_specs=[pl.BlockSpec(memory_space=pltpu.SMEM)] * 2
        + [pl.BlockSpec(memory_space=pltpu.VMEM)] * 3,
        out_specs=[pl.BlockSpec(memory_space=pltpu.VMEM)] * 2,
        scratch_shapes=[
            pltpu.SMEM((BLOCKS,), jnp.int32),
            pltpu.VMEM((KEYS, 256), jnp.bfloat16),
            pltpu.VMEM((KEYS, 256), jnp.bfloat16),
        ],
        name="attend",
    )(positions, lengths, queries, gathered, gain)


CUTS = ((2, (0, 1), 0, 1536), (1, (0, 2), 1536, 1280), (0, (1, 2), 2816, 1280))
WIDEST = 1536
PLANE = 32
HALF = 16


def shift(ctx, exp, steps):
    dz, dy, dx, dcore = steps
    return (
        ((ctx // 4 + dz) % 4) * 4 + (ctx % 4 + dy) % 4,
        ((exp // 2 + dx) % 4) * 2 + (exp % 2 + dcore) % 2,
    )


def line_steps(axis, step):
    steps = [0, 0, 0, 0]
    steps[axis] = step
    return steps


def plane_steps(plane, slot, sign):
    steps = [0, 0, 0, slot // HALF]
    for axis, step in zip(plane, ((slot // 4) % 4, slot % 4)):
        steps[axis] = step if sign > 0 else (4 - step) % 4
    return steps


def ones(hit):
    return hit.astype(jnp.float32).astype(jnp.bfloat16)


def main_hits(slots, count):
    wide = jnp.broadcast_to(slots[:, None, :], (count, 8, TOK))
    return (wide == lax.broadcasted_iota(jnp.int32, (count, 8, TOK), 1)).reshape(count * 8, TOK)


def extra_hits(slots, count, source):
    wide = jnp.broadcast_to(slots[:, None, :], (count, 8, TOK))
    row = lax.broadcasted_iota(jnp.int32, (count, 8, TOK), 1)
    hit = (wide == 8 + row % 2) & (row // 2 == source)
    return hit.reshape(count * 8, TOK)


def extra_order_y():
    row = lax.broadcasted_iota(jnp.int32, (64, 64), 0)
    column = lax.broadcasted_iota(jnp.int32, (64, 64), 1)
    z, y, x, i = row // 32, (row // 8) % 4, (row // 2) % 4, row % 2
    return ones(column == z * 32 + x * 8 + y * 2 + i)


def extra_order_z(half):
    row = lax.broadcasted_iota(jnp.int32, (64, 128), 0)
    column = lax.broadcasted_iota(jnp.int32, (64, 128), 1)
    z, y, x, i = row // 32 + 2 * half, (row // 8) % 4, (row // 2) % 4, row % 2
    return ones(column == (y * 4 + x) * 8 + z * 2 + i)


def moe_kernel(
    routes_ref,
    gates_ref,
    att_ref,
    norm_ref,
    gate_hbm,
    up_hbm,
    down_hbm,
    out_ref,
    arrived_0,
    arrived_1,
    arrived_2,
    returned_0,
    returned_1,
    returned_2,
    gate_ref,
    up_ref,
    down_ref,
    message_0,
    message_1,
    message_2,
    stage_0,
    stage_1,
    stage_2,
    shared_0,
    shared_1,
    shared_2,
    collect_0,
    collect_1,
    collect_2,
    all_routes,
    all_gates,
    slot_ref,
    weight_ref,
    part_sum,
    sum_ref,
    line_send,
    line_recv,
    send_out,
    recv_out,
    send_back,
    recv_back,
    local_sem,
):
    arrived = (arrived_0, arrived_1, arrived_2)
    returned = (returned_0, returned_1, returned_2)
    message = (message_0, message_1, message_2)
    stage = (stage_0, stage_1, stage_2)
    shared = (shared_0, shared_1, shared_2)
    collect = (collect_0, collect_1, collect_2)
    ctx = lax.axis_index("ctx")
    exp = lax.axis_index("exp")
    place = (ctx // 4, ctx % 4, exp // 2)
    core = exp % 2

    loads = [
        pltpu.make_async_copy(source, target, local_sem.at[i])
        for i, (source, target) in enumerate(
            ((gate_hbm, gate_ref), (up_hbm, up_ref), (down_hbm, down_ref))
        )
    ]

    barrier = pltpu.get_barrier_semaphore()

    def greet(delta, carry):
        dz, dy, dx, dcore = delta // 32, (delta // 8) % 4, (delta // 2) % 4, delta % 2

        @pl.when(dz * dy * dx == 0)
        def _():
            pl.semaphore_signal(
                barrier,
                inc=1,
                device_id=shift(ctx, exp, (dz, dy, dx, dcore)),
                device_id_type=MESH,
            )

        return carry

    lax.fori_loop(1, N_DEV, greet, 0)

    for cut, (axis, plane, first, width) in enumerate(CUTS):
        shared[cut][0] = norm_ref[:, first : first + width]
        all_routes[cut, 0] = routes_ref[...]
        all_gates[cut, 0] = gates_ref[...]
    sum_ref[...] = att_ref[...].astype(jnp.float32)
    pl.semaphore_wait(barrier, 2 * (64 - 27) - 1)

    def line_copy(cut, kind, step):
        ref = (all_routes.at[cut], all_gates.at[cut], shared[cut])[kind]
        return pltpu.make_async_remote_copy(
            src_ref=ref.at[0],
            dst_ref=ref.at[step],
            send_sem=line_send.at[cut, kind, step],
            recv_sem=line_recv.at[cut, kind, step],
            device_id=shift(ctx, exp, line_steps(CUTS[cut][0], step)),
            device_id_type=MESH,
        )

    line_copies = [
        (cut, kind, step) for kind in range(3) for step in (1, 3, 2) for cut in range(3)
    ]
    for which in line_copies:
        line_copy(*which).start()
    for load in loads:
        load.start()

    earlier = ones(
        lax.broadcasted_iota(jnp.int32, (TOK, TOK), 0)
        < lax.broadcasted_iota(jnp.int32, (TOK, TOK), 1)
    )
    for cut, (axis, plane, first, width) in enumerate(CUTS):
        for step in (1, 3, 2):
            line_copy(cut, 0, step).wait()
            line_copy(cut, 1, step).wait()
        slot = lax.broadcasted_iota(jnp.int32, (PLANE, TOK), 0)
        at = [jnp.full((PLANE, TOK), 0, jnp.int32) + coordinate for coordinate in place]
        at[plane[0]] = (at[plane[0]] + (slot // 4) % 4) % 4
        at[plane[1]] = (at[plane[1]] + slot % 4) % 4
        ids = (at[0] * 4 + at[1]) * 8 + at[2] * 2 + (core + slot // HALF) % 2

        def tables(source, carry, cut=cut, ids=ids):
            named = jnp.zeros((PLANE, TOK), jnp.float32)
            weight = jnp.zeros((PLANE, TOK), jnp.float32)
            for k in range(8):
                hit = all_routes[cut, source, k : k + 1, :] == ids
                named = named + hit.astype(jnp.float32)
                weight = weight + jnp.where(hit, all_gates[cut, source, k : k + 1, :], 0.0)
            ranks = jnp.dot(
                named.astype(jnp.bfloat16), earlier, preferred_element_type=jnp.float32
            )
            slot_ref[cut, source] = jnp.where(named > 0.5, ranks.astype(jnp.int32), -1)
            weight_ref[cut, source] = weight
            return carry

        lax.fori_loop(0, 4, tables, 0)

    for cut, (axis, plane, first, width) in enumerate(CUTS):
        for step in (1, 3, 2):
            line_copy(cut, 2, step).wait()
        extra = jnp.zeros((PLANE * 8, width), jnp.float32)
        for source in range(4):
            slots = slot_ref[cut, source]
            tokens = shared[cut][source]
            rows = jnp.dot(
                ones(main_hits(slots, PLANE)), tokens, preferred_element_type=jnp.float32
            )
            message[cut][:, source] = rows.astype(jnp.bfloat16).reshape(PLANE, 8, width)
            extra = extra + jnp.dot(
                ones(extra_hits(slots, PLANE, source)),
                tokens,
                preferred_element_type=jnp.float32,
            )
        message[cut][:, 4] = extra.astype(jnp.bfloat16).reshape(PLANE, 8, width)

    def outward(cut, slot):
        return pltpu.make_async_remote_copy(
            src_ref=message[cut].at[slot],
            dst_ref=arrived[cut].at[slot],
            send_sem=send_out.at[cut, slot],
            recv_sem=recv_out.at[cut, slot],
            device_id=shift(ctx, exp, plane_steps(CUTS[cut][1], slot, 1)),
            device_id_type=MESH,
        )

    def homeward(cut, slot):
        return pltpu.make_async_remote_copy(
            src_ref=message[cut].at[slot],
            dst_ref=returned[cut].at[slot],
            send_sem=send_back.at[cut, slot],
            recv_sem=recv_back.at[cut, slot],
            device_id=shift(ctx, exp, plane_steps(CUTS[cut][1], slot, -1)),
            device_id_type=MESH,
        )

    def own_copy(cut, target, sem):
        return pltpu.make_async_copy(message[cut].at[0], target[cut].at[0], local_sem.at[sem])

    def own_out(cut):
        return own_copy(cut, arrived, 3 + cut)

    def own_back(cut):
        return own_copy(cut, returned, 6 + cut)

    def each(half, cuts, remote, own):
        def one(k, carry):
            slot = half * HALF + (k * 7) % HALF

            @pl.when(slot > 0)
            def _():
                for cut in cuts:
                    remote(cut, slot)

            @pl.when(slot == 0)
            def _():
                for cut in cuts:
                    own(cut)

            return carry

        lax.fori_loop(0, HALF, one, 0)

    every = (0, 1, 2)
    for half in range(2):
        each(half, every, lambda cut, slot: outward(cut, slot).start(), lambda cut: own_out(cut).start())
    for load in loads:
        load.wait()

    def fetch(source, cut, half):
        return pltpu.make_async_copy(
            source[cut].at[pl.ds(half * HALF, HALF)], stage[cut], local_sem.at[9 + cut]
        )

    def expert_half(half, carry):
        each(half, every, lambda cut, slot: outward(cut, slot).wait(), lambda cut: own_out(cut).wait())
        for cut in every:
            fetch(arrived, cut, half).start()
        for cut in every:
            fetch(arrived, cut, half).wait()

        def two_z(pair, inner):
            near = pl.ds(pl.multiple_of(pair * 8, 8), 8)
            order_y = extra_order_y()
            order_z = extra_order_z(pair)
            gate = jnp.zeros((320, HID), jnp.float32)
            up = jnp.zeros((320, HID), jnp.float32)
            for cut, (axis, plane, first, width) in enumerate(CUTS):
                if cut == 0:
                    pieces = [
                        stage[0][pl.ds(pair * 8 + k, 1), 0:4].reshape(32, width) for k in range(8)
                    ]
                    pieces.append(stage[0][near, 4].reshape(64, width))
                elif cut == 1:
                    pieces = [
                        stage[1][pl.ds(pair * 8 + z * 4, 4), y].reshape(32, width)
                        for z in range(2)
                        for y in range(4)
                    ]
                    packed = stage[1][near, 4].reshape(64, width)
                    extra = jnp.dot(order_y, packed, preferred_element_type=jnp.float32)
                    pieces.append(extra.astype(jnp.bfloat16))
                else:
                    pieces = [
                        stage[2][:, pair * 2 + z].reshape(128, width) for z in range(2)
                    ]
                    packed = stage[2][:, 4].reshape(128, width)
                    extra = jnp.dot(order_z, packed, preferred_element_type=jnp.float32)
                    pieces.append(extra.astype(jnp.bfloat16))
                rows = jnp.concatenate(pieces, axis=0)
                span = slice(first, first + width)
                gate = gate + jnp.dot(rows, gate_ref[span, :], preferred_element_type=jnp.float32)
                up = up + jnp.dot(rows, up_ref[span, :], preferred_element_type=jnp.float32)
            hidden = (gate / (1.0 + jnp.exp(-gate)) * up).astype(jnp.bfloat16)
            base = half * HALF
            for cut, (axis, plane, first, width) in enumerate(CUTS):
                result = jnp.dot(
                    hidden, down_ref[:, first : first + width], preferred_element_type=jnp.float32
                ).astype(jnp.bfloat16)
                last = result[256:]
                if cut == 0:
                    for k in range(8):
                        message[0][pl.ds(base + pair * 8 + k, 1), 0:4] = result[
                            k * 32 : k * 32 + 32
                        ].reshape(1, 4, 8, width)
                    message[0][pl.ds(base + pair * 8, 8), 4] = last.reshape(8, 8, width)
                elif cut == 1:
                    for z in range(2):
                        for y in range(4):
                            k = z * 4 + y
                            message[1][pl.ds(base + pair * 8 + z * 4, 4), y] = result[
                                k * 32 : k * 32 + 32
                            ].reshape(4, 8, width)
                    spread = lax.dot_general(
                        order_y, last, (((0,), (0,)), ((), ())), preferred_element_type=jnp.float32
                    )
                    message[1][pl.ds(base + pair * 8, 8), 4] = spread.astype(
                        jnp.bfloat16
                    ).reshape(8, 8, width)
                else:
                    whole = pl.ds(base, HALF)
                    for z in range(2):
                        message[2][whole, pair * 2 + z] = result[
                            z * 128 : z * 128 + 128
                        ].reshape(HALF, 8, width)
                    spread = lax.dot_general(
                        order_z, last, (((0,), (0,)), ((), ())), preferred_element_type=jnp.float32
                    ).astype(jnp.bfloat16).reshape(HALF, 8, width)
                    held = message[2][whole, 4]
                    message[2][whole, 4] = spread + jnp.where(
                        pair == 0, jnp.zeros_like(held), held
                    )
            return inner

        lax.fori_loop(0, 2, two_z, 0)
        each(half, every, lambda cut, slot: homeward(cut, slot).start(), lambda cut: own_back(cut).start())
        return carry

    lax.fori_loop(0, 2, expert_half, 0)

    def collect_copy(cut, source):
        axis = CUTS[cut][0]
        return pltpu.make_async_remote_copy(
            src_ref=shared[cut].at[source],
            dst_ref=collect[cut].at[source - 1],
            send_sem=line_send.at[cut, 3, source],
            recv_sem=line_recv.at[cut, 3, source],
            device_id=shift(ctx, exp, line_steps(axis, 4 - source)),
            device_id_type=MESH,
        )

    def answers(cut, half):
        width = CUTS[cut][3]
        each(half, (cut,), lambda c, slot: homeward(c, slot).wait(), lambda c: own_back(c).wait())
        copy = fetch(returned, cut, half)
        copy.start()
        copy.wait()

        def one(source, carry):
            span = pl.ds(half * HALF, HALF)
            slots = slot_ref[cut, source, span, :]
            weights = jnp.broadcast_to(
                weight_ref[cut, source, span, :][:, None, :], (HALF, 8, TOK)
            ).reshape(HALF * 8, TOK)
            value = jnp.concatenate(
                [
                    jnp.where(main_hits(slots, HALF), weights, 0.0),
                    jnp.where(extra_hits(slots, HALF, source), weights, 0.0),
                ],
                axis=0,
            )
            high = value.astype(jnp.bfloat16)
            low = (value - high.astype(jnp.float32)).astype(jnp.bfloat16)
            factors = jnp.concatenate([high, low], axis=1)
            rows = jnp.concatenate(
                [
                    stage[cut][:, source].reshape(HALF * 8, width),
                    stage[cut][:, 4].reshape(HALF * 8, width),
                ],
                axis=0,
            )
            both = lax.dot_general(
                factors, rows, (((0,), (0,)), ((), ())), preferred_element_type=jnp.float32
            )
            total = both[:TOK] + both[TOK:]
            if half == 0:
                part_sum[source, :, 0:width] = total
            else:
                part_sum[source, :, 0:width] = part_sum[source, :, 0:width] + total
            return carry

        lax.fori_loop(0, 4, one, 0)

    for cut, (axis, plane, first, width) in enumerate(CUTS):
        answers(cut, 0)
        answers(cut, 1)
        for source in (1, 3, 2):
            shared[cut][source] = part_sum[source, :, 0:width].astype(jnp.bfloat16)
            collect_copy(cut, source).start()
        span = slice(first, first + width)
        sum_ref[:, span] = sum_ref[:, span] + part_sum[0, :, 0:width]
    for cut, (axis, plane, first, width) in enumerate(CUTS):
        span = slice(first, first + width)
        for source in (1, 3, 2):
            collect_copy(cut, source).wait()
        total = sum_ref[:, span]
        for source in range(3):
            total = total + collect[cut][source].astype(jnp.float32)
        out_ref[:, span] = total.astype(jnp.bfloat16)


def moe(routes, gates, attended, normed, gate, up, down):
    vmem = pl.BlockSpec(memory_space=pltpu.VMEM)
    hbm = pl.BlockSpec(memory_space=pltpu.HBM)
    widths = [width for axis, plane, first, width in CUTS]
    wire = [(PLANE, 5, 8, width) for width in widths]
    return pl.pallas_call(
        moe_kernel,
        out_shape=[jax.ShapeDtypeStruct((TOK, D), jnp.bfloat16)]
        + [jax.ShapeDtypeStruct(shape, jnp.bfloat16) for shape in wire] * 2,
        in_specs=[vmem] * 4 + [hbm] * 3,
        out_specs=[vmem] + [hbm] * 6,
        scratch_shapes=[
            pltpu.VMEM((D, HID), jnp.bfloat16),
            pltpu.VMEM((D, HID), jnp.bfloat16),
            pltpu.VMEM((HID, D), jnp.bfloat16),
        ]
        + [pltpu.VMEM(shape, jnp.bfloat16) for shape in wire]
        + [pltpu.VMEM((HALF, 5, 8, width), jnp.bfloat16) for width in widths]
        + [pltpu.VMEM((4, TOK, width), jnp.bfloat16) for width in widths]
        + [pltpu.VMEM((3, TOK, width), jnp.bfloat16) for width in widths]
        + [
            pltpu.VMEM((3, 4, 8, TOK), jnp.int32),
            pltpu.VMEM((3, 4, 8, TOK), jnp.float32),
            pltpu.VMEM((3, 4, PLANE, TOK), jnp.int32),
            pltpu.VMEM((3, 4, PLANE, TOK), jnp.float32),
            pltpu.VMEM((4, TOK, WIDEST), jnp.float32),
            pltpu.VMEM((TOK, D), jnp.float32),
            pltpu.SemaphoreType.DMA((3, 4, 4)),
            pltpu.SemaphoreType.DMA((3, 4, 4)),
            pltpu.SemaphoreType.DMA((3, PLANE)),
            pltpu.SemaphoreType.DMA((3, PLANE)),
            pltpu.SemaphoreType.DMA((3, PLANE)),
            pltpu.SemaphoreType.DMA((3, PLANE)),
            pltpu.SemaphoreType.DMA((12,)),
        ],
        compiler_params=pltpu.CompilerParams(
            collective_id=1, has_side_effects=True, vmem_limit_bytes=62 << 20
        ),
        name="moe",
    )(routes, gates, attended, normed, gate, up, down)[0]


def local(
    query_states,
    key_states,
    value_states,
    positions,
    lengths,
    routes,
    gate_weights,
    norm_gain,
    gate_proj,
    up_proj,
    down_proj,
):
    gathered = gather_keys(key_states[0], value_states[0])
    attended, normed = attend(
        positions, lengths, query_states[0], gathered, norm_gain.reshape(1, D)
    )
    out = moe(
        routes[0].T,
        gate_weights[0].T,
        attended,
        normed,
        gate_proj[0],
        up_proj[0],
        down_proj[0],
    )
    return out[None]


def solution(mesh):
    in_specs = (
        P("exp", "ctx", None),
        P("exp", "ctx", None),
        P("exp", "ctx", None),
        P("exp", None),
        P("exp", None),
        P("exp", "ctx", None),
        P("exp", "ctx", None),
        P(),
        P(("ctx", "exp"), None, None),
        P(("ctx", "exp"), None, None),
        P(("ctx", "exp"), None, None),
    )
    out_specs = P("exp", "ctx", None)
    return jax.shard_map(local, mesh=mesh, in_specs=in_specs, out_specs=out_specs, check_vma=False)
```

```python
import functools
import math

import jax
import jax.numpy as jnp
from jax import lax
from jax.experimental import pallas as pl
from jax.experimental.pallas import tpu as pltpu
from jax.sharding import PartitionSpec as P

QH = 32
HD = 128
D = 4096
HID = 768
TOK = 128
N_CTX = 16
N_DEV = 128
SEQ = 2048
DOCS = 16
RUN = 64
BLOCKS = SEQ // RUN
WINDOW = 10
KEYS = WINDOW * RUN
MESH = pl.DeviceIdType.MESH

neg_large = -1e30
norm_eps = 1e-06


def gather_kernel(k_ref, v_ref, out_ref, send_sem, recv_sem, local_sem):
    ctx = lax.axis_index("ctx")
    exp = lax.axis_index("exp")

    def along(axis, origin, step):
        oz, oy = origin // 4, origin % 4
        if axis == 0:
            return oz * 4 + (oy + step) % 4
        return ((oz + step) % 4) * 4 + oy

    barrier = pltpu.get_barrier_semaphore()
    for axis in range(2):
        for step in range(1, 4):
            pl.semaphore_signal(
                barrier, inc=1, device_id=(along(axis, ctx, step), exp), device_id_type=MESH
            )
    pl.semaphore_wait(barrier, 6)

    started = []
    for which in range(2):
        for step in range(1, 4):
            sent = pltpu.make_async_remote_copy(
                src_ref=(k_ref, v_ref)[which],
                dst_ref=out_ref.at[ctx, which],
                send_sem=send_sem.at[which, 0, step],
                recv_sem=recv_sem.at[which, 0, step],
                device_id=(along(which, ctx, step), exp),
                device_id_type=MESH,
            )
            sent.start()
            started.append(sent)

    def pass_on(which, first):
        origin = along(which, ctx, 4 - first) if first else ctx
        for step in range(1, 4):
            sent = pltpu.make_async_remote_copy(
                src_ref=out_ref.at[origin, which] if first else (k_ref, v_ref)[which],
                dst_ref=out_ref.at[origin, which],
                send_sem=send_sem.at[which, 1 + first, step],
                recv_sem=recv_sem.at[which, 1 + first, step],
                device_id=(along(1 - which, ctx, step), exp),
                device_id_type=MESH,
            )
            sent.start()
            started.append(sent)

    for which in range(2):
        pass_on(which, 0)
    own = [
        pltpu.make_async_copy(source, out_ref.at[ctx, which], local_sem.at[which])
        for which, source in enumerate((k_ref, v_ref))
    ]
    for sent in own:
        sent.start()
    for first in (1, 3, 2):
        for which in range(2):
            started[which * 3 + first - 1].wait_recv()
            pass_on(which, first)
    for index, sent in enumerate(started):
        sent.wait_send()
        if index >= 6:
            sent.wait_recv()
    for sent in own:
        sent.wait()


def gather_keys(keys, values):
    return pl.pallas_call(
        gather_kernel,
        out_shape=jax.ShapeDtypeStruct((N_CTX, 2, TOK, 256), jnp.bfloat16),
        in_specs=[pl.BlockSpec(memory_space=pltpu.VMEM)] * 2,
        out_specs=pl.BlockSpec(memory_space=pltpu.VMEM),
        scratch_shapes=[
            pltpu.SemaphoreType.DMA((2, 5, 4)),
            pltpu.SemaphoreType.DMA((2, 5, 4)),
            pltpu.SemaphoreType.DMA((2,)),
        ],
        compiler_params=pltpu.CompilerParams(collective_id=0, has_side_effects=True),
        name="gather_keys",
    )(keys, values)


def attend_kernel(
    pos_ref, len_ref, q_ref, kv_ref, gain_ref, att_ref, norm_ref, where_ref, k_win, v_win
):
    ctx = lax.axis_index("ctx")
    for block in range(BLOCKS):
        where_ref[pos_ref[0, RUN * block] // RUN] = block
    ends = []
    total = jnp.int32(0)
    for doc in range(DOCS):
        total = total + len_ref[0, doc]
        ends.append(total)

    def one_run(run, carry):
        first_block = pos_ref[0, ctx * TOK + run * RUN] // RUN
        for step in range(WINDOW):
            block = where_ref[jnp.maximum(first_block - (WINDOW - 1) + step, 0)]
            rows = pl.ds(pl.multiple_of((block % 2) * RUN, RUN), RUN)
            k_win[pl.ds(step * RUN, RUN), :] = kv_ref[block // 2, 0, rows, :]
            v_win[pl.ds(step * RUN, RUN), :] = kv_ref[block // 2, 1, rows, :]
        own = first_block * RUN + lax.broadcasted_iota(jnp.int32, (RUN, 1), 0)
        start = jnp.zeros((RUN, 1), jnp.int32)
        for end in ends:
            start = jnp.maximum(start, jnp.where(own >= end, end, 0))
        places = (first_block - (WINDOW - 1)) * RUN + lax.broadcasted_iota(
            jnp.int32, (RUN, KEYS), 1
        )
        visible = (places >= start) & (places <= own)
        tokens = pl.ds(pl.multiple_of(run * RUN, RUN), RUN)

        def eight_heads(pair, inner):
            chains = []
            for part in (2 * pair, 2 * pair + 1):
                lanes = pl.ds(pl.multiple_of((part // 4) * HD, HD), HD)
                queries = jnp.concatenate(
                    [
                        q_ref[tokens, pl.ds(pl.multiple_of((part * 4 + i) * HD, HD), HD)]
                        for i in range(4)
                    ],
                    axis=0,
                )
                scores = lax.dot_general(
                    queries,
                    k_win[:, lanes],
                    (((1,), (1,)), ((), ())),
                    preferred_element_type=jnp.float32,
                )
                chains.append((part, lanes, scores))
            for part, lanes, scores in chains:
                scores = jnp.where(visible[None], scores.reshape(4, RUN, KEYS), neg_large)
                maxima = jnp.max(scores, axis=2, keepdims=True)
                probs = jnp.exp((scores - maxima) * (1.0 / math.sqrt(HD)))
                totals = jnp.sum(probs, axis=2, keepdims=True)
                summed = jnp.dot(
                    probs.reshape(4 * RUN, KEYS).astype(jnp.bfloat16),
                    v_win[:, lanes],
                    preferred_element_type=jnp.float32,
                )
                result = (summed.reshape(4, RUN, HD) / totals).astype(jnp.bfloat16)
                for i in range(4):
                    att_ref[
                        tokens, pl.ds(pl.multiple_of((part * 4 + i) * HD, HD), HD)
                    ] = result[i]
            return inner

        lax.fori_loop(0, QH // 8, eight_heads, 0)
        wide = att_ref[tokens, :].astype(jnp.float32)
        scale = lax.rsqrt(jnp.mean(wide * wide, axis=1, keepdims=True) + norm_eps)
        norm_ref[tokens, :] = (wide * scale * gain_ref[...]).astype(jnp.bfloat16)
        return carry

    lax.fori_loop(0, TOK // RUN, one_run, 0)


def attend(positions, lengths, queries, gathered, gain):
    return pl.pallas_call(
        attend_kernel,
        out_shape=[jax.ShapeDtypeStruct((TOK, D), jnp.bfloat16)] * 2,
        in_specs=[pl.BlockSpec(memory_space=pltpu.SMEM)] * 2
        + [pl.BlockSpec(memory_space=pltpu.VMEM)] * 3,
        out_specs=[pl.BlockSpec(memory_space=pltpu.VMEM)] * 2,
        scratch_shapes=[
            pltpu.SMEM((BLOCKS,), jnp.int32),
            pltpu.VMEM((KEYS, 256), jnp.bfloat16),
            pltpu.VMEM((KEYS, 256), jnp.bfloat16),
        ],
        name="attend",
    )(positions, lengths, queries, gathered, gain)


CUTS = ((2, (0, 1), 0, 1536), (1, (0, 2), 1536, 1280), (0, (1, 2), 2816, 1280))
PLANE = 32
HALF = 16


def shift(ctx, exp, steps):
    dz, dy, dx, dcore = steps
    return (
        ((ctx // 4 + dz) % 4) * 4 + (ctx % 4 + dy) % 4,
        ((exp // 2 + dx) % 4) * 2 + (exp % 2 + dcore) % 2,
    )


def line_steps(axis, step):
    steps = [0, 0, 0, 0]
    steps[axis] = step
    return steps


def plane_steps(plane, slot, sign):
    steps = [0, 0, 0, slot // HALF]
    for axis, step in zip(plane, ((slot // 4) % 4, slot % 4)):
        steps[axis] = step if sign > 0 else (4 - step) % 4
    return steps


def ones(hit):
    return hit.astype(jnp.float32).astype(jnp.bfloat16)


def main_hits(slots, count):
    wide = jnp.broadcast_to(slots[:, None, :], (count, 8, TOK))
    return (wide == lax.broadcasted_iota(jnp.int32, (count, 8, TOK), 1)).reshape(count * 8, TOK)


def extra_hits(slots, count, source):
    wide = jnp.broadcast_to(slots[:, None, :], (count, 8, TOK))
    row = lax.broadcasted_iota(jnp.int32, (count, 8, TOK), 1)
    hit = (wide == 8 + row % 2) & (row // 2 == source)
    return hit.reshape(count * 8, TOK)


def extra_order_y():
    row = lax.broadcasted_iota(jnp.int32, (64, 64), 0)
    column = lax.broadcasted_iota(jnp.int32, (64, 64), 1)
    z, y, x, i = row // 32, (row // 8) % 4, (row // 2) % 4, row % 2
    return ones(column == z * 32 + x * 8 + y * 2 + i)


def extra_order_z(half):
    row = lax.broadcasted_iota(jnp.int32, (64, 128), 0)
    column = lax.broadcasted_iota(jnp.int32, (64, 128), 1)
    z, y, x, i = row // 32 + 2 * half, (row // 8) % 4, (row // 2) % 4, row % 2
    return ones(column == (y * 4 + x) * 8 + z * 2 + i)


def moe_kernel(
    routes_ref,
    gates_ref,
    att_ref,
    norm_ref,
    gate_hbm,
    up_hbm,
    down_hbm,
    out_ref,
    arrived_0,
    arrived_1,
    arrived_2,
    returned_0,
    returned_1,
    returned_2,
    gate_ref,
    up_ref,
    down_ref,
    message_0,
    message_1,
    message_2,
    stage_0,
    stage_1,
    stage_2,
    shared_0,
    shared_1,
    shared_2,
    collect_0,
    collect_1,
    collect_2,
    all_routes,
    all_gates,
    slot_ref,
    weight_ref,
    part_sum,
    line_send,
    line_recv,
    send_out,
    recv_out,
    send_back,
    recv_back,
    local_sem,
):
    arrived = (arrived_0, arrived_1, arrived_2)
    returned = (returned_0, returned_1, returned_2)
    message = (message_0, message_1, message_2)
    stage = (stage_0, stage_1, stage_2)
    shared = (shared_0, shared_1, shared_2)
    collect = (collect_0, collect_1, collect_2)
    ctx = lax.axis_index("ctx")
    exp = lax.axis_index("exp")
    place = (ctx // 4, ctx % 4, exp // 2)
    core = exp % 2

    loads = [
        pltpu.make_async_copy(source, target, local_sem.at[i])
        for i, (source, target) in enumerate(
            ((gate_hbm, gate_ref), (up_hbm, up_ref), (down_hbm, down_ref))
        )
    ]

    barrier = pltpu.get_barrier_semaphore()

    def greet(delta, carry):
        dz, dy, dx, dcore = delta // 32, (delta // 8) % 4, (delta // 2) % 4, delta % 2

        @pl.when(dz * dy * dx == 0)
        def _():
            pl.semaphore_signal(
                barrier,
                inc=1,
                device_id=shift(ctx, exp, (dz, dy, dx, dcore)),
                device_id_type=MESH,
            )

        return carry

    lax.fori_loop(1, N_DEV, greet, 0)

    for cut, (axis, plane, first, width) in enumerate(CUTS):
        shared[cut][0] = norm_ref[:, first : first + width]
        all_routes[cut, 0] = routes_ref[...]
        all_gates[cut, 0] = gates_ref[...]
    pl.semaphore_wait(barrier, 2 * (64 - 27) - 1)

    def line_copy(cut, kind, step):
        ref = (all_routes.at[cut], all_gates.at[cut], shared[cut])[kind]
        return pltpu.make_async_remote_copy(
            src_ref=ref.at[0],
            dst_ref=ref.at[step],
            send_sem=line_send.at[cut, kind, step],
            recv_sem=line_recv.at[cut, kind, step],
            device_id=shift(ctx, exp, line_steps(CUTS[cut][0], step)),
            device_id_type=MESH,
        )

    line_copies = [
        (cut, kind, step) for kind in range(3) for step in (1, 3, 2) for cut in range(3)
    ]
    for which in line_copies:
        line_copy(*which).start()
    for load in loads:
        load.start()

    earlier = ones(
        lax.broadcasted_iota(jnp.int32, (TOK, TOK), 0)
        < lax.broadcasted_iota(jnp.int32, (TOK, TOK), 1)
    )
    def tables(cut, source):
        plane = CUTS[cut][1]
        slot = lax.broadcasted_iota(jnp.int32, (PLANE, TOK), 0)
        at = [jnp.full((PLANE, TOK), 0, jnp.int32) + coordinate for coordinate in place]
        at[plane[0]] = (at[plane[0]] + (slot // 4) % 4) % 4
        at[plane[1]] = (at[plane[1]] + slot % 4) % 4
        ids = (at[0] * 4 + at[1]) * 8 + at[2] * 2 + (core + slot // HALF) % 2
        named = jnp.zeros((PLANE, TOK), jnp.float32)
        weight = jnp.zeros((PLANE, TOK), jnp.float32)
        for k in range(8):
            hit = all_routes[cut, source, k : k + 1, :] == ids
            named = named + hit.astype(jnp.float32)
            weight = weight + jnp.where(hit, all_gates[cut, source, k : k + 1, :], 0.0)
        ranks = jnp.dot(named.astype(jnp.bfloat16), earlier, preferred_element_type=jnp.float32)
        slot_ref[cut, source] = jnp.where(named > 0.5, ranks.astype(jnp.int32), -1)
        weight_ref[cut, source] = weight

    def pack_main(cut, source):
        rows = jnp.dot(
            ones(main_hits(slot_ref[cut, source], PLANE)),
            shared[cut][source],
            preferred_element_type=jnp.float32,
        )
        message[cut][:, source] = rows.astype(jnp.bfloat16).reshape(PLANE, 8, CUTS[cut][3])

    def pack_extra(cut):
        width = CUTS[cut][3]
        hits = jnp.concatenate(
            [ones(extra_hits(slot_ref[cut, source], PLANE, source)) for source in range(4)], axis=1
        )
        rows = jnp.dot(
            hits, shared[cut][...].reshape(4 * TOK, width), preferred_element_type=jnp.float32
        )
        message[cut][:, 4] = rows.astype(jnp.bfloat16).reshape(PLANE, 8, width)

    def sources(cut, first, last, work):
        def one(source, carry):
            work(cut, source)
            return carry

        lax.fori_loop(first, last, one, 0)

    for cut in range(3):
        tables(cut, 0)
        pack_main(cut, 0)
    for cut in range(3):
        for step in (1, 3, 2):
            line_copy(cut, 0, step).wait()
            line_copy(cut, 1, step).wait()
        sources(cut, 1, 4, tables)

    def outward(cut, slot):
        return pltpu.make_async_remote_copy(
            src_ref=message[cut].at[slot],
            dst_ref=arrived[cut].at[slot],
            send_sem=send_out.at[cut, slot],
            recv_sem=recv_out.at[cut, slot],
            device_id=shift(ctx, exp, plane_steps(CUTS[cut][1], slot, 1)),
            device_id_type=MESH,
        )

    def homeward(cut, slot):
        return pltpu.make_async_remote_copy(
            src_ref=message[cut].at[slot],
            dst_ref=returned[cut].at[slot],
            send_sem=send_back.at[cut, slot],
            recv_sem=recv_back.at[cut, slot],
            device_id=shift(ctx, exp, plane_steps(CUTS[cut][1], slot, -1)),
            device_id_type=MESH,
        )

    def own_copy(cut, target, sem):
        return pltpu.make_async_copy(message[cut].at[0], target[cut].at[0], local_sem.at[sem])

    def own_out(cut):
        return own_copy(cut, arrived, 3 + cut)

    def own_back(cut):
        return own_copy(cut, returned, 6 + cut)

    def each(half, cuts, remote, own, begin=0, end=HALF):
        def one(k, carry):
            slot = half * HALF + (k * 7) % HALF

            @pl.when(slot > 0)
            def _():
                for cut in cuts:
                    remote(cut, slot)

            @pl.when(slot == 0)
            def _():
                for cut in cuts:
                    own(cut)

            return carry

        lax.fori_loop(begin, end, one, 0)

    every = (0, 1, 2)
    def send(cut, slot):
        outward(cut, slot).start()

    def send_own(cut):
        own_out(cut).start()

    early = 4
    for cut in every:
        for step in (1, 3, 2):
            line_copy(cut, 2, step).wait()
        sources(cut, 1, 4, pack_main)
        pack_extra(cut)
        each(0, (cut,), send, send_own, 0, early)
    each(0, every, send, send_own, early, HALF)
    each(1, every, send, send_own)
    for load in loads:
        load.wait()

    def fetch(source, cut, half):
        return pltpu.make_async_copy(
            source[cut].at[pl.ds(half * HALF, HALF)], stage[cut], local_sem.at[9 + cut]
        )

    def expert_half(half, carry):
        each(half, every, lambda cut, slot: outward(cut, slot).wait(), lambda cut: own_out(cut).wait())
        for cut in every:
            fetch(arrived, cut, half).start()
        for cut in every:
            fetch(arrived, cut, half).wait()

        def two_z(pair, inner):
            near = pl.ds(pl.multiple_of(pair * 8, 8), 8)
            order_y = extra_order_y()
            order_z = extra_order_z(pair)
            gate = jnp.zeros((320, HID), jnp.float32)
            up = jnp.zeros((320, HID), jnp.float32)
            for cut, (axis, plane, first, width) in enumerate(CUTS):
                if cut == 0:
                    pieces = [
                        stage[0][pl.ds(pair * 8 + k, 1), 0:4].reshape(32, width) for k in range(8)
                    ]
                    pieces.append(stage[0][near, 4].reshape(64, width))
                elif cut == 1:
                    pieces = [
                        stage[1][pl.ds(pair * 8 + z * 4, 4), y].reshape(32, width)
                        for z in range(2)
                        for y in range(4)
                    ]
                    packed = stage[1][near, 4].reshape(64, width)
                    extra = jnp.dot(order_y, packed, preferred_element_type=jnp.float32)
                    pieces.append(extra.astype(jnp.bfloat16))
                else:
                    pieces = [
                        stage[2][:, pair * 2 + z].reshape(128, width) for z in range(2)
                    ]
                    packed = stage[2][:, 4].reshape(128, width)
                    extra = jnp.dot(order_z, packed, preferred_element_type=jnp.float32)
                    pieces.append(extra.astype(jnp.bfloat16))
                rows = jnp.concatenate(pieces, axis=0)
                span = slice(first, first + width)
                gate = gate + jnp.dot(rows, gate_ref[span, :], preferred_element_type=jnp.float32)
                up = up + jnp.dot(rows, up_ref[span, :], preferred_element_type=jnp.float32)
            hidden = (gate / (1.0 + jnp.exp(-gate)) * up).astype(jnp.bfloat16)
            base = half * HALF
            for cut, (axis, plane, first, width) in enumerate(CUTS):
                result = jnp.dot(
                    hidden, down_ref[:, first : first + width], preferred_element_type=jnp.float32
                ).astype(jnp.bfloat16)
                last = result[256:]
                if cut == 0:
                    for k in range(8):
                        message[0][pl.ds(base + pair * 8 + k, 1), 0:4] = result[
                            k * 32 : k * 32 + 32
                        ].reshape(1, 4, 8, width)
                    message[0][pl.ds(base + pair * 8, 8), 4] = last.reshape(8, 8, width)
                elif cut == 1:
                    for z in range(2):
                        for y in range(4):
                            k = z * 4 + y
                            message[1][pl.ds(base + pair * 8 + z * 4, 4), y] = result[
                                k * 32 : k * 32 + 32
                            ].reshape(4, 8, width)
                    spread = lax.dot_general(
                        order_y, last, (((0,), (0,)), ((), ())), preferred_element_type=jnp.float32
                    )
                    message[1][pl.ds(base + pair * 8, 8), 4] = spread.astype(
                        jnp.bfloat16
                    ).reshape(8, 8, width)
                else:
                    whole = pl.ds(base, HALF)
                    for z in range(2):
                        message[2][whole, pair * 2 + z] = result[
                            z * 128 : z * 128 + 128
                        ].reshape(HALF, 8, width)
                    spread = lax.dot_general(
                        order_z, last, (((0,), (0,)), ((), ())), preferred_element_type=jnp.float32
                    ).astype(jnp.bfloat16).reshape(HALF, 8, width)
                    held = message[2][whole, 4]
                    message[2][whole, 4] = spread + jnp.where(
                        pair == 0, jnp.zeros_like(held), held
                    )

            def answer(k, inner):
                slot = base + pair * 8 + (k * 3) % 8

                @pl.when(slot > 0)
                def _():
                    homeward(0, slot).start()
                    homeward(1, slot).start()

                @pl.when(slot == 0)
                def _():
                    own_back(0).start()
                    own_back(1).start()

                return inner

            lax.fori_loop(0, 8, answer, 0)
            return inner

        lax.fori_loop(0, 2, two_z, 0)
        each(half, (2,), lambda cut, slot: homeward(cut, slot).start(), lambda cut: own_back(cut).start())
        return carry

    lax.fori_loop(0, 2, expert_half, 0)

    def collect_copy(cut, source):
        axis = CUTS[cut][0]
        return pltpu.make_async_remote_copy(
            src_ref=shared[cut].at[source],
            dst_ref=collect[cut].at[source - 1],
            send_sem=line_send.at[cut, 3, source],
            recv_sem=line_recv.at[cut, 3, source],
            device_id=shift(ctx, exp, line_steps(axis, 4 - source)),
            device_id_type=MESH,
        )

    def answers(cut, half):
        first, width = CUTS[cut][2:]
        each(half, (cut,), lambda c, slot: homeward(c, slot).wait(), lambda c: own_back(c).wait())
        copy = fetch(returned, cut, half)
        copy.start()
        copy.wait()

        def one(source, carry):
            span = pl.ds(half * HALF, HALF)
            slots = slot_ref[cut, source, span, :]
            weights = jnp.broadcast_to(
                weight_ref[cut, source, span, :][:, None, :], (HALF, 8, TOK)
            ).reshape(HALF * 8, TOK)
            value = jnp.concatenate(
                [
                    jnp.where(main_hits(slots, HALF), weights, 0.0),
                    jnp.where(extra_hits(slots, HALF, source), weights, 0.0),
                ],
                axis=0,
            )
            high = value.astype(jnp.bfloat16)
            low = (value - high.astype(jnp.float32)).astype(jnp.bfloat16)
            factors = jnp.concatenate([high, low], axis=1)
            rows = jnp.concatenate(
                [
                    stage[cut][:, source].reshape(HALF * 8, width),
                    stage[cut][:, 4].reshape(HALF * 8, width),
                ],
                axis=0,
            )
            both = lax.dot_general(
                factors, rows, (((0,), (0,)), ((), ())), preferred_element_type=jnp.float32
            )
            total = both[:TOK] + both[TOK:]
            if half == 0:
                part_sum[source, :, first : first + width] = total
            else:
                part_sum[source, :, first : first + width] += total
            return carry

        lax.fori_loop(0, 4, one, 0)

    for cut in every:
        answers(cut, 0)
    for cut, (axis, plane, first, width) in enumerate(CUTS):
        answers(cut, 1)
        for source in (1, 3, 2):
            shared[cut][source] = part_sum[source, :, first : first + width].astype(jnp.bfloat16)
            collect_copy(cut, source).start()
    for cut, (axis, plane, first, width) in enumerate(CUTS):
        span = slice(first, first + width)
        total = att_ref[:, span].astype(jnp.float32) + part_sum[0, :, span]
        for source in (1, 3, 2):
            collect_copy(cut, source).wait()
            total = total + collect[cut][source - 1].astype(jnp.float32)
        out_ref[:, span] = total.astype(jnp.bfloat16)


def moe(routes, gates, attended, normed, gate, up, down):
    vmem = pl.BlockSpec(memory_space=pltpu.VMEM)
    hbm = pl.BlockSpec(memory_space=pltpu.HBM)
    widths = [width for axis, plane, first, width in CUTS]
    wire = [(PLANE, 5, 8, width) for width in widths]
    return pl.pallas_call(
        moe_kernel,
        out_shape=[jax.ShapeDtypeStruct((TOK, D), jnp.bfloat16)]
        + [jax.ShapeDtypeStruct(shape, jnp.bfloat16) for shape in wire] * 2,
        in_specs=[vmem] * 4 + [hbm] * 3,
        out_specs=[vmem] + [hbm] * 6,
        scratch_shapes=[
            pltpu.VMEM((D, HID), jnp.bfloat16),
            pltpu.VMEM((D, HID), jnp.bfloat16),
            pltpu.VMEM((HID, D), jnp.bfloat16),
        ]
        + [pltpu.VMEM(shape, jnp.bfloat16) for shape in wire]
        + [pltpu.VMEM((HALF, 5, 8, width), jnp.bfloat16) for width in widths]
        + [pltpu.VMEM((4, TOK, width), jnp.bfloat16) for width in widths]
        + [pltpu.VMEM((3, TOK, width), jnp.bfloat16) for width in widths]
        + [
            pltpu.VMEM((3, 4, 8, TOK), jnp.int32),
            pltpu.VMEM((3, 4, 8, TOK), jnp.float32),
            pltpu.VMEM((3, 4, PLANE, TOK), jnp.int32),
            pltpu.VMEM((3, 4, PLANE, TOK), jnp.float32),
            pltpu.VMEM((4, TOK, D), jnp.float32),
            pltpu.SemaphoreType.DMA((3, 4, 4)),
            pltpu.SemaphoreType.DMA((3, 4, 4)),
            pltpu.SemaphoreType.DMA((3, PLANE)),
            pltpu.SemaphoreType.DMA((3, PLANE)),
            pltpu.SemaphoreType.DMA((3, PLANE)),
            pltpu.SemaphoreType.DMA((3, PLANE)),
            pltpu.SemaphoreType.DMA((12,)),
        ],
        compiler_params=pltpu.CompilerParams(
            collective_id=1, has_side_effects=True, vmem_limit_bytes=62 << 20
        ),
        name="moe",
    )(routes, gates, attended, normed, gate, up, down)[0]


def local(
    query_states,
    key_states,
    value_states,
    positions,
    lengths,
    routes,
    gate_weights,
    norm_gain,
    gate_proj,
    up_proj,
    down_proj,
):
    gathered = gather_keys(key_states[0], value_states[0])
    attended, normed = attend(
        positions, lengths, query_states[0], gathered, norm_gain.reshape(1, D)
    )
    out = moe(
        routes[0].T,
        gate_weights[0].T,
        attended,
        normed,
        gate_proj[0],
        up_proj[0],
        down_proj[0],
    )
    return out[None]


def solution(mesh):
    in_specs = (
        P("exp", "ctx", None),
        P("exp", "ctx", None),
        P("exp", "ctx", None),
        P("exp", None),
        P("exp", None),
        P("exp", "ctx", None),
        P("exp", "ctx", None),
        P(),
        P(("ctx", "exp"), None, None),
        P(("ctx", "exp"), None, None),
        P(("ctx", "exp"), None, None),
    )
    out_specs = P("exp", "ctx", None)
    return jax.shard_map(local, mesh=mesh, in_specs=in_specs, out_specs=out_specs, check_vma=False)
```

```python
import functools
import math

import jax
import jax.numpy as jnp
from jax import lax
from jax.experimental import pallas as pl
from jax.experimental.pallas import tpu as pltpu
from jax.sharding import PartitionSpec as P

QH = 32
HD = 128
D = 4096
HID = 768
TOK = 128
N_CTX = 16
N_DEV = 128
SEQ = 2048
DOCS = 16
RUN = 64
BLOCKS = SEQ // RUN
WINDOW = 10
KEYS = WINDOW * RUN
MESH = pl.DeviceIdType.MESH

neg_large = -1e30
norm_eps = 1e-06


def gather_kernel(k_ref, v_ref, all_k, all_v, send_sem, recv_sem, local_sem):
    out = (all_k, all_v)
    ctx = lax.axis_index("ctx")
    exp = lax.axis_index("exp")

    def along(axis, origin, step):
        oz, oy = origin // 4, origin % 4
        if axis == 0:
            return oz * 4 + (oy + step) % 4
        return ((oz + step) % 4) * 4 + oy

    barrier = pltpu.get_barrier_semaphore()
    for axis in range(2):
        for step in range(1, 4):
            pl.semaphore_signal(
                barrier, inc=1, device_id=(along(axis, ctx, step), exp), device_id_type=MESH
            )
    pl.semaphore_wait(barrier, 6)

    started = []
    for which in range(2):
        for step in range(1, 4):
            sent = pltpu.make_async_remote_copy(
                src_ref=(k_ref, v_ref)[which],
                dst_ref=out[which].at[ctx],
                send_sem=send_sem.at[which, 0, step],
                recv_sem=recv_sem.at[which, 0, step],
                device_id=(along(which, ctx, step), exp),
                device_id_type=MESH,
            )
            sent.start()
            started.append(sent)

    def pass_on(which, first):
        origin = along(which, ctx, 4 - first) if first else ctx
        for step in range(1, 4):
            sent = pltpu.make_async_remote_copy(
                src_ref=out[which].at[origin] if first else (k_ref, v_ref)[which],
                dst_ref=out[which].at[origin],
                send_sem=send_sem.at[which, 1 + first, step],
                recv_sem=recv_sem.at[which, 1 + first, step],
                device_id=(along(1 - which, ctx, step), exp),
                device_id_type=MESH,
            )
            sent.start()
            started.append(sent)

    for which in range(2):
        pass_on(which, 0)
    own = [
        pltpu.make_async_copy(source, out[which].at[ctx], local_sem.at[which])
        for which, source in enumerate((k_ref, v_ref))
    ]
    for sent in own:
        sent.start()
    for first in (1, 3, 2):
        for which in range(2):
            started[which * 3 + first - 1].wait_recv()
            pass_on(which, first)
    for index, sent in enumerate(started):
        sent.wait_send()
        if index >= 6:
            sent.wait_recv()
    for sent in own:
        sent.wait()


def gather_keys(keys, values):
    return pl.pallas_call(
        gather_kernel,
        out_shape=[jax.ShapeDtypeStruct((N_CTX, TOK, 256), jnp.bfloat16)] * 2,
        in_specs=[pl.BlockSpec(memory_space=pltpu.VMEM)] * 2,
        out_specs=[pl.BlockSpec(memory_space=pltpu.VMEM)] * 2,
        scratch_shapes=[
            pltpu.SemaphoreType.DMA((2, 5, 4)),
            pltpu.SemaphoreType.DMA((2, 5, 4)),
            pltpu.SemaphoreType.DMA((2,)),
        ],
        compiler_params=pltpu.CompilerParams(collective_id=0, has_side_effects=True),
        name="gather_keys",
    )(keys, values)


CUTS = ((2, (0, 1), 0, 1536), (1, (0, 2), 1536, 1280), (0, (1, 2), 2816, 1280))
PLANE = 32
HALF = 16


def shift(ctx, exp, steps):
    dz, dy, dx, dcore = steps
    return (
        ((ctx // 4 + dz) % 4) * 4 + (ctx % 4 + dy) % 4,
        ((exp // 2 + dx) % 4) * 2 + (exp % 2 + dcore) % 2,
    )


def line_steps(axis, step):
    steps = [0, 0, 0, 0]
    steps[axis] = step
    return steps


def plane_steps(plane, slot, sign):
    steps = [0, 0, 0, slot // HALF]
    for axis, step in zip(plane, ((slot // 4) % 4, slot % 4)):
        steps[axis] = step if sign > 0 else (4 - step) % 4
    return steps


def ones(hit):
    return hit.astype(jnp.float32).astype(jnp.bfloat16)


def main_hits(slots, count):
    wide = jnp.broadcast_to(slots[:, None, :], (count, 8, TOK))
    return (wide == lax.broadcasted_iota(jnp.int32, (count, 8, TOK), 1)).reshape(count * 8, TOK)


def extra_hits(slots, count, source):
    wide = jnp.broadcast_to(slots[:, None, :], (count, 8, TOK))
    row = lax.broadcasted_iota(jnp.int32, (count, 8, TOK), 1)
    hit = (wide == 8 + row % 2) & (row // 2 == source)
    return hit.reshape(count * 8, TOK)


def extra_order_y():
    row = lax.broadcasted_iota(jnp.int32, (64, 64), 0)
    column = lax.broadcasted_iota(jnp.int32, (64, 64), 1)
    z, y, x, i = row // 32, (row // 8) % 4, (row // 2) % 4, row % 2
    return ones(column == z * 32 + x * 8 + y * 2 + i)


def extra_order_z(half):
    row = lax.broadcasted_iota(jnp.int32, (64, 128), 0)
    column = lax.broadcasted_iota(jnp.int32, (64, 128), 1)
    z, y, x, i = row // 32 + 2 * half, (row // 8) % 4, (row // 2) % 4, row % 2
    return ones(column == (y * 4 + x) * 8 + z * 2 + i)


def moe_kernel(
    pos_ref,
    len_ref,
    q_ref,
    k_ref,
    v_ref,
    gain_ref,
    routes_ref,
    gates_ref,
    gate_hbm,
    up_hbm,
    down_hbm,
    out_ref,
    arrived_0,
    arrived_1,
    arrived_2,
    returned_0,
    returned_1,
    returned_2,
    att_ref,
    k_win,
    v_win,
    gate_ref,
    up_ref,
    down_ref,
    message_0,
    message_1,
    message_2,
    stage_0,
    stage_1,
    stage_2,
    shared_0,
    shared_1,
    shared_2,
    collect_0,
    collect_1,
    collect_2,
    all_routes,
    all_gates,
    slot_ref,
    weight_ref,
    part_sum,
    line_send,
    line_recv,
    send_out,
    recv_out,
    send_back,
    recv_back,
    local_sem,
):
    arrived = (arrived_0, arrived_1, arrived_2)
    returned = (returned_0, returned_1, returned_2)
    message = (message_0, message_1, message_2)
    stage = (stage_0, stage_1, stage_2)
    shared = (shared_0, shared_1, shared_2)
    collect = (collect_0, collect_1, collect_2)
    ctx = lax.axis_index("ctx")
    exp = lax.axis_index("exp")
    place = (ctx // 4, ctx % 4, exp // 2)
    core = exp % 2

    loads = [
        pltpu.make_async_copy(source, target, local_sem.at[i])
        for i, (source, target) in enumerate(
            ((gate_hbm, gate_ref), (up_hbm, up_ref), (down_hbm, down_ref))
        )
    ]

    barrier = pltpu.get_barrier_semaphore()

    def greet(delta, carry):
        dz, dy, dx, dcore = delta // 32, (delta // 8) % 4, (delta // 2) % 4, delta % 2

        @pl.when(dz * dy * dx == 0)
        def _():
            pl.semaphore_signal(
                barrier,
                inc=1,
                device_id=shift(ctx, exp, (dz, dy, dx, dcore)),
                device_id_type=MESH,
            )

        return carry

    lax.fori_loop(1, N_DEV, greet, 0)

    blocks_at = [pos_ref[0, RUN * block] // RUN for block in range(BLOCKS)]
    ends = []
    total = jnp.int32(0)
    for doc in range(DOCS):
        total = total + len_ref[0, doc]
        ends.append(total)

    def attend_run(run):
        first_block = pos_ref[0, ctx * TOK + run * RUN] // RUN

        def window(step, carry):
            wanted = jnp.maximum(first_block - (WINDOW - 1) + step, 0)
            block = jnp.int32(0)
            for index, here in enumerate(blocks_at):
                block = jnp.where(here == wanted, index, block)
            rows = pl.ds(pl.multiple_of(step * RUN, RUN), RUN)
            k_win[rows, :] = k_ref[block]
            v_win[rows, :] = v_ref[block]
            return carry

        lax.fori_loop(0, WINDOW, window, 0)
        own = first_block * RUN + lax.broadcasted_iota(jnp.int32, (RUN, 1), 0)
        start = jnp.zeros((RUN, 1), jnp.int32)
        for end in ends:
            start = jnp.maximum(start, jnp.where(own >= end, end, 0))
        places = (first_block - (WINDOW - 1)) * RUN + lax.broadcasted_iota(
            jnp.int32, (RUN, KEYS), 1
        )
        visible = (places >= start) & (places <= own)
        tokens = slice(run * RUN, run * RUN + RUN)

        def eight_heads(pair, inner):
            chains = []
            for part in (2 * pair, 2 * pair + 1):
                lanes = pl.ds(pl.multiple_of((part // 4) * HD, HD), HD)
                queries = jnp.concatenate(
                    [
                        q_ref[tokens, pl.ds(pl.multiple_of((part * 4 + i) * HD, HD), HD)]
                        for i in range(4)
                    ],
                    axis=0,
                )
                scores = lax.dot_general(
                    queries,
                    k_win[:, lanes],
                    (((1,), (1,)), ((), ())),
                    preferred_element_type=jnp.float32,
                )
                chains.append((part, lanes, scores))
            for part, lanes, scores in chains:
                scores = jnp.where(visible[None], scores.reshape(4, RUN, KEYS), neg_large)
                maxima = jnp.max(scores, axis=2, keepdims=True)
                probs = jnp.exp((scores - maxima) * (1.0 / math.sqrt(HD)))
                totals = jnp.sum(probs, axis=2, keepdims=True)
                summed = jnp.dot(
                    probs.reshape(4 * RUN, KEYS).astype(jnp.bfloat16),
                    v_win[:, lanes],
                    preferred_element_type=jnp.float32,
                )
                result = (summed.reshape(4, RUN, HD) / totals).astype(jnp.bfloat16)
                for i in range(4):
                    att_ref[
                        tokens, pl.ds(pl.multiple_of((part * 4 + i) * HD, HD), HD)
                    ] = result[i]
            return inner

        lax.fori_loop(0, QH // 8, eight_heads, 0)
        wide = att_ref[tokens, :].astype(jnp.float32)
        scale = lax.rsqrt(jnp.mean(wide * wide, axis=1, keepdims=True) + norm_eps)
        for cut, (axis, plane, first, width) in enumerate(CUTS):
            span = slice(first, first + width)
            shared[cut][0, tokens, :] = (wide[:, span] * scale * gain_ref[:, span]).astype(
                jnp.bfloat16
            )

    def line_copy(cut, kind, step):
        if kind < 2:
            ref = (all_routes, all_gates)[kind].at[cut]
            source, target = ref.at[0], ref.at[step]
        else:
            run = pl.ds((kind - 2) * RUN, RUN)
            source, target = shared[cut].at[0, run], shared[cut].at[step, run]
        return pltpu.make_async_remote_copy(
            src_ref=source,
            dst_ref=target,
            send_sem=line_send.at[cut, kind, step],
            recv_sem=line_recv.at[cut, kind, step],
            device_id=shift(ctx, exp, line_steps(CUTS[cut][0], step)),
            device_id_type=MESH,
        )

    def share(kinds):
        for kind in kinds:
            for step in (1, 3, 2):
                for cut in range(3):
                    line_copy(cut, kind, step).start()

    for cut in range(3):
        all_routes[cut, 0] = routes_ref[...]
        all_gates[cut, 0] = gates_ref[...]
    attend_run(0)
    pl.semaphore_wait(barrier, 2 * (64 - 27) - 1)
    share((0, 1, 2))
    attend_run(1)
    share((3,))
    for load in loads:
        load.start()

    earlier = ones(
        lax.broadcasted_iota(jnp.int32, (TOK, TOK), 0)
        < lax.broadcasted_iota(jnp.int32, (TOK, TOK), 1)
    )
    def tables(cut, source):
        plane = CUTS[cut][1]
        slot = lax.broadcasted_iota(jnp.int32, (PLANE, TOK), 0)
        at = [jnp.full((PLANE, TOK), 0, jnp.int32) + coordinate for coordinate in place]
        at[plane[0]] = (at[plane[0]] + (slot // 4) % 4) % 4
        at[plane[1]] = (at[plane[1]] + slot % 4) % 4
        ids = (at[0] * 4 + at[1]) * 8 + at[2] * 2 + (core + slot // HALF) % 2
        named = jnp.zeros((PLANE, TOK), jnp.float32)
        weight = jnp.zeros((PLANE, TOK), jnp.float32)
        for k in range(8):
            hit = all_routes[cut, source, k : k + 1, :] == ids
            named = named + hit.astype(jnp.float32)
            weight = weight + jnp.where(hit, all_gates[cut, source, k : k + 1, :], 0.0)
        ranks = jnp.dot(named.astype(jnp.bfloat16), earlier, preferred_element_type=jnp.float32)
        slot_ref[cut, source] = jnp.where(named > 0.5, ranks.astype(jnp.int32), -1)
        weight_ref[cut, source] = weight

    def pack_main(cut, source):
        rows = jnp.dot(
            ones(main_hits(slot_ref[cut, source], PLANE)),
            shared[cut][source],
            preferred_element_type=jnp.float32,
        )
        message[cut][:, source] = rows.astype(jnp.bfloat16).reshape(PLANE, 8, CUTS[cut][3])

    def pack_extra(cut):
        width = CUTS[cut][3]
        hits = jnp.concatenate(
            [ones(extra_hits(slot_ref[cut, source], PLANE, source)) for source in range(4)], axis=1
        )
        rows = jnp.dot(
            hits, shared[cut][...].reshape(4 * TOK, width), preferred_element_type=jnp.float32
        )
        message[cut][:, 4] = rows.astype(jnp.bfloat16).reshape(PLANE, 8, width)

    def sources(cut, first, last, work):
        def one(source, carry):
            work(cut, source)
            return carry

        lax.fori_loop(first, last, one, 0)

    for cut in range(3):
        tables(cut, 0)
        pack_main(cut, 0)
    for cut in range(3):
        for step in (1, 3, 2):
            line_copy(cut, 0, step).wait()
            line_copy(cut, 1, step).wait()
        sources(cut, 1, 4, tables)

    def outward(cut, slot):
        return pltpu.make_async_remote_copy(
            src_ref=message[cut].at[slot],
            dst_ref=arrived[cut].at[slot],
            send_sem=send_out.at[cut, slot],
            recv_sem=recv_out.at[cut, slot],
            device_id=shift(ctx, exp, plane_steps(CUTS[cut][1], slot, 1)),
            device_id_type=MESH,
        )

    def homeward(cut, slot):
        return pltpu.make_async_remote_copy(
            src_ref=message[cut].at[slot],
            dst_ref=returned[cut].at[slot],
            send_sem=send_back.at[cut, slot],
            recv_sem=recv_back.at[cut, slot],
            device_id=shift(ctx, exp, plane_steps(CUTS[cut][1], slot, -1)),
            device_id_type=MESH,
        )

    def own_copy(cut, target, sem):
        return pltpu.make_async_copy(message[cut].at[0], target[cut].at[0], local_sem.at[sem])

    def own_out(cut):
        return own_copy(cut, arrived, 3 + cut)

    def own_back(cut):
        return own_copy(cut, returned, 6 + cut)

    def each(half, cuts, remote, own, begin=0, end=HALF):
        def one(k, carry):
            slot = half * HALF + (k * 7) % HALF

            @pl.when(slot > 0)
            def _():
                for cut in cuts:
                    remote(cut, slot)

            @pl.when(slot == 0)
            def _():
                for cut in cuts:
                    own(cut)

            return carry

        lax.fori_loop(begin, end, one, 0)

    every = (0, 1, 2)
    def send(cut, slot):
        outward(cut, slot).start()

    def send_own(cut):
        own_out(cut).start()

    early = 4
    for step in (1, 3):
        for cut in every:
            line_copy(cut, 2, step).wait()
            line_copy(cut, 3, step).wait()
            pack_main(cut, step)
    for cut in every:
        line_copy(cut, 2, 2).wait()
        line_copy(cut, 3, 2).wait()
        pack_main(cut, 2)
        pack_extra(cut)
        each(0, (cut,), send, send_own, 0, early)
    each(0, every, send, send_own, early, HALF)
    each(1, every, send, send_own)
    for load in loads:
        load.wait()

    def fetch(source, cut, half):
        return pltpu.make_async_copy(
            source[cut].at[pl.ds(half * HALF, HALF)], stage[cut], local_sem.at[9 + cut]
        )

    def expert_half(half, carry):
        each(half, every, lambda cut, slot: outward(cut, slot).wait(), lambda cut: own_out(cut).wait())
        for cut in every:
            fetch(arrived, cut, half).start()
        for cut in every:
            fetch(arrived, cut, half).wait()

        def two_z(pair, inner):
            near = pl.ds(pl.multiple_of(pair * 8, 8), 8)
            order_y = extra_order_y()
            order_z = extra_order_z(pair)
            gate = jnp.zeros((320, HID), jnp.float32)
            up = jnp.zeros((320, HID), jnp.float32)
            for cut, (axis, plane, first, width) in enumerate(CUTS):
                if cut == 0:
                    pieces = [
                        stage[0][pl.ds(pair * 8 + k, 1), 0:4].reshape(32, width) for k in range(8)
                    ]
                    pieces.append(stage[0][near, 4].reshape(64, width))
                elif cut == 1:
                    pieces = [
                        stage[1][pl.ds(pair * 8 + z * 4, 4), y].reshape(32, width)
                        for z in range(2)
                        for y in range(4)
                    ]
                    packed = stage[1][near, 4].reshape(64, width)
                    extra = jnp.dot(order_y, packed, preferred_element_type=jnp.float32)
                    pieces.append(extra.astype(jnp.bfloat16))
                else:
                    pieces = [
                        stage[2][:, pair * 2 + z].reshape(128, width) for z in range(2)
                    ]
                    packed = stage[2][:, 4].reshape(128, width)
                    extra = jnp.dot(order_z, packed, preferred_element_type=jnp.float32)
                    pieces.append(extra.astype(jnp.bfloat16))
                rows = jnp.concatenate(pieces, axis=0)
                span = slice(first, first + width)
                gate = gate + jnp.dot(rows, gate_ref[span, :], preferred_element_type=jnp.float32)
                up = up + jnp.dot(rows, up_ref[span, :], preferred_element_type=jnp.float32)
            hidden = (gate / (1.0 + jnp.exp(-gate)) * up).astype(jnp.bfloat16)
            base = half * HALF
            for cut, (axis, plane, first, width) in enumerate(CUTS):
                result = jnp.dot(
                    hidden, down_ref[:, first : first + width], preferred_element_type=jnp.float32
                ).astype(jnp.bfloat16)
                last = result[256:]
                if cut == 0:
                    for k in range(8):
                        message[0][pl.ds(base + pair * 8 + k, 1), 0:4] = result[
                            k * 32 : k * 32 + 32
                        ].reshape(1, 4, 8, width)
                    message[0][pl.ds(base + pair * 8, 8), 4] = last.reshape(8, 8, width)
                elif cut == 1:
                    for z in range(2):
                        for y in range(4):
                            k = z * 4 + y
                            message[1][pl.ds(base + pair * 8 + z * 4, 4), y] = result[
                                k * 32 : k * 32 + 32
                            ].reshape(4, 8, width)
                    spread = lax.dot_general(
                        order_y, last, (((0,), (0,)), ((), ())), preferred_element_type=jnp.float32
                    )
                    message[1][pl.ds(base + pair * 8, 8), 4] = spread.astype(
                        jnp.bfloat16
                    ).reshape(8, 8, width)
                else:
                    whole = pl.ds(base, HALF)
                    for z in range(2):
                        message[2][whole, pair * 2 + z] = result[
                            z * 128 : z * 128 + 128
                        ].reshape(HALF, 8, width)
                    spread = lax.dot_general(
                        order_z, last, (((0,), (0,)), ((), ())), preferred_element_type=jnp.float32
                    ).astype(jnp.bfloat16).reshape(HALF, 8, width)
                    held = message[2][whole, 4]
                    message[2][whole, 4] = spread + jnp.where(
                        pair == 0, jnp.zeros_like(held), held
                    )

            def answer(k, inner):
                slot = base + pair * 8 + (k * 3) % 8
                later = base + ((2 * k) * 7) % HALF
                last = base + ((2 * k + 1) * 7) % HALF

                @pl.when(pair == 1)
                def _():
                    @pl.when(later > 0)
                    def _():
                        homeward(2, later).start()

                    @pl.when(later == 0)
                    def _():
                        own_back(2).start()

                    homeward(2, last).start()

                @pl.when(slot > 0)
                def _():
                    homeward(0, slot).start()
                    homeward(1, slot).start()

                @pl.when(slot == 0)
                def _():
                    own_back(0).start()
                    own_back(1).start()

                return inner

            lax.fori_loop(0, 8, answer, 0)
            return inner

        lax.fori_loop(0, 2, two_z, 0)
        return carry

    lax.fori_loop(0, 2, expert_half, 0)

    def collect_copy(cut, source):
        axis = CUTS[cut][0]
        return pltpu.make_async_remote_copy(
            src_ref=shared[cut].at[source],
            dst_ref=collect[cut].at[source - 1],
            send_sem=line_send.at[cut, 4, source],
            recv_sem=line_recv.at[cut, 4, source],
            device_id=shift(ctx, exp, line_steps(axis, 4 - source)),
            device_id_type=MESH,
        )

    def answers(cut, half):
        first, width = CUTS[cut][2:]
        fetch(returned, cut, half).wait()

        def one(source, carry):
            span = pl.ds(half * HALF, HALF)
            slots = slot_ref[cut, source, span, :]
            weights = jnp.broadcast_to(
                weight_ref[cut, source, span, :][:, None, :], (HALF, 8, TOK)
            ).reshape(HALF * 8, TOK)
            value = jnp.concatenate(
                [
                    jnp.where(main_hits(slots, HALF), weights, 0.0),
                    jnp.where(extra_hits(slots, HALF, source), weights, 0.0),
                ],
                axis=0,
            )
            high = value.astype(jnp.bfloat16)
            low = (value - high.astype(jnp.float32)).astype(jnp.bfloat16)
            factors = jnp.concatenate([high, low], axis=1)
            rows = jnp.concatenate(
                [
                    stage[cut][:, source].reshape(HALF * 8, width),
                    stage[cut][:, 4].reshape(HALF * 8, width),
                ],
                axis=0,
            )
            both = lax.dot_general(
                factors, rows, (((0,), (0,)), ((), ())), preferred_element_type=jnp.float32
            )
            total = both[:TOK] + both[TOK:]
            if half == 0:
                part_sum[source, :, first : first + width] = total
            else:
                part_sum[source, :, first : first + width] += total
            return carry

        lax.fori_loop(0, 4, one, 0)

    def arrive(cut, half):
        each(half, (cut,), lambda c, slot: homeward(c, slot).wait(), lambda c: own_back(c).wait())
        fetch(returned, cut, half).start()

    for cut in every:
        arrive(cut, 0)
    for cut in every:
        answers(cut, 0)
    arrive(0, 1)
    arrive(1, 1)
    for cut, (axis, plane, first, width) in enumerate(CUTS):
        answers(cut, 1)
        for source in (1, 3, 2):
            shared[cut][source] = part_sum[source, :, first : first + width].astype(jnp.bfloat16)
            collect_copy(cut, source).start()
        if cut == 0:
            arrive(2, 1)
    for cut, (axis, plane, first, width) in enumerate(CUTS):
        span = slice(first, first + width)
        total = att_ref[:, span].astype(jnp.float32) + part_sum[0, :, span]
        for source in (1, 3, 2):
            collect_copy(cut, source).wait()
            total = total + collect[cut][source - 1].astype(jnp.float32)
        out_ref[:, span] = total.astype(jnp.bfloat16)


def moe(positions, lengths, queries, keys, values, gain, routes, gates, gate, up, down):
    vmem = pl.BlockSpec(memory_space=pltpu.VMEM)
    hbm = pl.BlockSpec(memory_space=pltpu.HBM)
    widths = [width for axis, plane, first, width in CUTS]
    wire = [(PLANE, 5, 8, width) for width in widths]
    return pl.pallas_call(
        moe_kernel,
        out_shape=[jax.ShapeDtypeStruct((TOK, D), jnp.bfloat16)]
        + [jax.ShapeDtypeStruct(shape, jnp.bfloat16) for shape in wire] * 2,
        in_specs=[pl.BlockSpec(memory_space=pltpu.SMEM)] * 2 + [vmem] * 6 + [hbm] * 3,
        out_specs=[vmem] + [hbm] * 6,
        scratch_shapes=[
            pltpu.VMEM((TOK, D), jnp.bfloat16),
            pltpu.VMEM((KEYS, 256), jnp.bfloat16),
            pltpu.VMEM((KEYS, 256), jnp.bfloat16),
            pltpu.VMEM((D, HID), jnp.bfloat16),
            pltpu.VMEM((D, HID), jnp.bfloat16),
            pltpu.VMEM((HID, D), jnp.bfloat16),
        ]
        + [pltpu.VMEM(shape, jnp.bfloat16) for shape in wire]
        + [pltpu.VMEM((HALF, 5, 8, width), jnp.bfloat16) for width in widths]
        + [pltpu.VMEM((4, TOK, width), jnp.bfloat16) for width in widths]
        + [pltpu.VMEM((3, TOK, width), jnp.bfloat16) for width in widths]
        + [
            pltpu.VMEM((3, 4, 8, TOK), jnp.int32),
            pltpu.VMEM((3, 4, 8, TOK), jnp.float32),
            pltpu.VMEM((3, 4, PLANE, TOK), jnp.int32),
            pltpu.VMEM((3, 4, PLANE, TOK), jnp.float32),
            pltpu.VMEM((4, TOK, D), jnp.float32),
            pltpu.SemaphoreType.DMA((3, 5, 4)),
            pltpu.SemaphoreType.DMA((3, 5, 4)),
            pltpu.SemaphoreType.DMA((3, PLANE)),
            pltpu.SemaphoreType.DMA((3, PLANE)),
            pltpu.SemaphoreType.DMA((3, PLANE)),
            pltpu.SemaphoreType.DMA((3, PLANE)),
            pltpu.SemaphoreType.DMA((12,)),
        ],
        compiler_params=pltpu.CompilerParams(
            collective_id=1, has_side_effects=True, vmem_limit_bytes=62 << 20
        ),
        name="moe",
    )(positions, lengths, queries, keys, values, gain, routes, gates, gate, up, down)[0]


def local(
    query_states,
    key_states,
    value_states,
    positions,
    lengths,
    routes,
    gate_weights,
    norm_gain,
    gate_proj,
    up_proj,
    down_proj,
):
    keys, values = gather_keys(key_states[0], value_states[0])
    out = moe(
        positions,
        lengths,
        query_states[0],
        keys.reshape(BLOCKS, RUN, 256),
        values.reshape(BLOCKS, RUN, 256),
        norm_gain.reshape(1, D),
        routes[0].T,
        gate_weights[0].T,
        gate_proj[0],
        up_proj[0],
        down_proj[0],
    )
    return out[None]


def solution(mesh):
    in_specs = (
        P("exp", "ctx", None),
        P("exp", "ctx", None),
        P("exp", "ctx", None),
        P("exp", None),
        P("exp", None),
        P("exp", "ctx", None),
        P("exp", "ctx", None),
        P(),
        P(("ctx", "exp"), None, None),
        P(("ctx", "exp"), None, None),
        P(("ctx", "exp"), None, None),
    )
    out_specs = P("exp", "ctx", None)
    return jax.shard_map(local, mesh=mesh, in_specs=in_specs, out_specs=out_specs, check_vma=False)
```

```python
import functools
import math

import jax
import jax.numpy as jnp
from jax import lax
from jax.experimental import pallas as pl
from jax.experimental.pallas import tpu as pltpu
from jax.sharding import PartitionSpec as P

QH = 32
HD = 128
D = 4096
HID = 768
TOK = 128
N_CTX = 16
N_DEV = 128
SEQ = 2048
DOCS = 16
RUN = 64
BLOCKS = SEQ // RUN
WINDOW = 10
KEYS = WINDOW * RUN
MESH = pl.DeviceIdType.MESH

neg_large = -1e30
norm_eps = 1e-06


def gather_kernel(k_ref, v_ref, all_k, all_v, send_sem, recv_sem, local_sem):
    out = (all_k, all_v)
    ctx = lax.axis_index("ctx")
    exp = lax.axis_index("exp")

    def along(axis, origin, step):
        oz, oy = origin // 4, origin % 4
        if axis == 0:
            return oz * 4 + (oy + step) % 4
        return ((oz + step) % 4) * 4 + oy

    barrier = pltpu.get_barrier_semaphore()
    for axis in range(2):
        for step in range(1, 4):
            pl.semaphore_signal(
                barrier, inc=1, device_id=(along(axis, ctx, step), exp), device_id_type=MESH
            )
    pl.semaphore_wait(barrier, 6)

    started = []
    for which in range(2):
        for step in range(1, 4):
            sent = pltpu.make_async_remote_copy(
                src_ref=(k_ref, v_ref)[which],
                dst_ref=out[which].at[ctx],
                send_sem=send_sem.at[which, 0, step],
                recv_sem=recv_sem.at[which, 0, step],
                device_id=(along(which, ctx, step), exp),
                device_id_type=MESH,
            )
            sent.start()
            started.append(sent)

    def pass_on(which, first):
        origin = along(which, ctx, 4 - first) if first else ctx
        for step in range(1, 4):
            sent = pltpu.make_async_remote_copy(
                src_ref=out[which].at[origin] if first else (k_ref, v_ref)[which],
                dst_ref=out[which].at[origin],
                send_sem=send_sem.at[which, 1 + first, step],
                recv_sem=recv_sem.at[which, 1 + first, step],
                device_id=(along(1 - which, ctx, step), exp),
                device_id_type=MESH,
            )
            sent.start()
            started.append(sent)

    for which in range(2):
        pass_on(which, 0)
    own = [
        pltpu.make_async_copy(source, out[which].at[ctx], local_sem.at[which])
        for which, source in enumerate((k_ref, v_ref))
    ]
    for sent in own:
        sent.start()
    for first in (1, 3, 2):
        for which in range(2):
            started[which * 3 + first - 1].wait_recv()
            pass_on(which, first)
    for index, sent in enumerate(started):
        sent.wait_send()
        if index >= 6:
            sent.wait_recv()
    for sent in own:
        sent.wait()


def gather_keys(keys, values):
    return pl.pallas_call(
        gather_kernel,
        out_shape=[jax.ShapeDtypeStruct((N_CTX, TOK, 256), jnp.bfloat16)] * 2,
        in_specs=[pl.BlockSpec(memory_space=pltpu.VMEM)] * 2,
        out_specs=[pl.BlockSpec(memory_space=pltpu.VMEM)] * 2,
        scratch_shapes=[
            pltpu.SemaphoreType.DMA((2, 5, 4)),
            pltpu.SemaphoreType.DMA((2, 5, 4)),
            pltpu.SemaphoreType.DMA((2,)),
        ],
        compiler_params=pltpu.CompilerParams(collective_id=0, has_side_effects=True),
        name="gather_keys",
    )(keys, values)


CUTS = ((2, (0, 1), 0, 1536), (1, (0, 2), 1536, 1280), (0, (1, 2), 2816, 1280))
PLANE = 32
HALF = 16


def shift(ctx, exp, steps):
    dz, dy, dx, dcore = steps
    return (
        ((ctx // 4 + dz) % 4) * 4 + (ctx % 4 + dy) % 4,
        ((exp // 2 + dx) % 4) * 2 + (exp % 2 + dcore) % 2,
    )


def line_steps(axis, step):
    steps = [0, 0, 0, 0]
    steps[axis] = step
    return steps


def plane_steps(plane, slot, sign):
    steps = [0, 0, 0, slot // HALF]
    for axis, step in zip(plane, ((slot // 4) % 4, slot % 4)):
        steps[axis] = step if sign > 0 else (4 - step) % 4
    return steps


def ones(hit):
    return hit.astype(jnp.float32).astype(jnp.bfloat16)


def main_hits(slots, count):
    wide = jnp.broadcast_to(slots[:, None, :], (count, 8, TOK))
    return (wide == lax.broadcasted_iota(jnp.int32, (count, 8, TOK), 1)).reshape(count * 8, TOK)


def extra_hits(slots, count, source):
    wide = jnp.broadcast_to(slots[:, None, :], (count, 8, TOK))
    row = lax.broadcasted_iota(jnp.int32, (count, 8, TOK), 1)
    hit = (wide == 8 + row % 2) & (row // 2 == source)
    return hit.reshape(count * 8, TOK)


def extra_order_y():
    row = lax.broadcasted_iota(jnp.int32, (64, 64), 0)
    column = lax.broadcasted_iota(jnp.int32, (64, 64), 1)
    z, y, x, i = row // 32, (row // 8) % 4, (row // 2) % 4, row % 2
    return ones(column == z * 32 + x * 8 + y * 2 + i)


def extra_order_z(half):
    row = lax.broadcasted_iota(jnp.int32, (64, 128), 0)
    column = lax.broadcasted_iota(jnp.int32, (64, 128), 1)
    z, y, x, i = row // 32 + 2 * half, (row // 8) % 4, (row // 2) % 4, row % 2
    return ones(column == (y * 4 + x) * 8 + z * 2 + i)


def moe_kernel(
    pos_ref,
    len_ref,
    q_ref,
    k_ref,
    v_ref,
    gain_ref,
    routes_ref,
    gates_ref,
    gate_hbm,
    up_hbm,
    down_hbm,
    out_ref,
    arrived_0,
    arrived_1,
    arrived_2,
    returned_0,
    returned_1,
    returned_2,
    att_ref,
    k_win,
    v_win,
    gate_ref,
    up_ref,
    down_ref,
    message_0,
    message_1,
    message_2,
    stage_0,
    stage_1,
    stage_2,
    shared_0,
    shared_1,
    shared_2,
    collect_0,
    collect_1,
    collect_2,
    all_routes,
    all_gates,
    slot_ref,
    weight_ref,
    part_sum,
    line_send,
    line_recv,
    send_out,
    recv_out,
    send_back,
    recv_back,
    local_sem,
):
    arrived = (arrived_0, arrived_1, arrived_2)
    returned = (returned_0, returned_1, returned_2)
    message = (message_0, message_1, message_2)
    stage = (stage_0, stage_1, stage_2)
    shared = (shared_0, shared_1, shared_2)
    collect = (collect_0, collect_1, collect_2)
    ctx = lax.axis_index("ctx")
    exp = lax.axis_index("exp")
    place = (ctx // 4, ctx % 4, exp // 2)
    core = exp % 2

    loads = [
        pltpu.make_async_copy(source, target, local_sem.at[i])
        for i, (source, target) in enumerate(
            ((gate_hbm, gate_ref), (up_hbm, up_ref), (down_hbm, down_ref))
        )
    ]

    barrier = pltpu.get_barrier_semaphore()

    def greet(delta, carry):
        dz, dy, dx, dcore = delta // 32, (delta // 8) % 4, (delta // 2) % 4, delta % 2

        @pl.when(dz * dy * dx == 0)
        def _():
            pl.semaphore_signal(
                barrier,
                inc=1,
                device_id=shift(ctx, exp, (dz, dy, dx, dcore)),
                device_id_type=MESH,
            )

        return carry

    lax.fori_loop(1, N_DEV, greet, 0)

    blocks_at = [pos_ref[0, RUN * block] // RUN for block in range(BLOCKS)]
    ends = []
    total = jnp.int32(0)
    for doc in range(DOCS):
        total = total + len_ref[0, doc]
        ends.append(total)

    def attend_run(run):
        first_block = pos_ref[0, ctx * TOK + run * RUN] // RUN

        def window(step, carry):
            wanted = jnp.maximum(first_block - (WINDOW - 1) + step, 0)
            block = jnp.int32(0)
            for index, here in enumerate(blocks_at):
                block = jnp.where(here == wanted, index, block)
            rows = pl.ds(pl.multiple_of(step * RUN, RUN), RUN)
            k_win[rows, :] = k_ref[block]
            v_win[rows, :] = v_ref[block]
            return carry

        lax.fori_loop(0, WINDOW, window, 0)
        own = first_block * RUN + lax.broadcasted_iota(jnp.int32, (RUN, 1), 0)
        start = jnp.zeros((RUN, 1), jnp.int32)
        for end in ends:
            start = jnp.maximum(start, jnp.where(own >= end, end, 0))
        places = (first_block - (WINDOW - 1)) * RUN + lax.broadcasted_iota(
            jnp.int32, (RUN, KEYS), 1
        )
        visible = (places >= start) & (places <= own)
        tokens = slice(run * RUN, run * RUN + RUN)

        def eight_heads(pair, inner):
            chains = []
            for part in (2 * pair, 2 * pair + 1):
                lanes = pl.ds(pl.multiple_of((part // 4) * HD, HD), HD)
                queries = jnp.concatenate(
                    [
                        q_ref[tokens, pl.ds(pl.multiple_of((part * 4 + i) * HD, HD), HD)]
                        for i in range(4)
                    ],
                    axis=0,
                )
                scores = lax.dot_general(
                    queries,
                    k_win[:, lanes],
                    (((1,), (1,)), ((), ())),
                    preferred_element_type=jnp.float32,
                )
                chains.append((part, lanes, scores))
            for part, lanes, scores in chains:
                scores = jnp.where(visible[None], scores.reshape(4, RUN, KEYS), neg_large)
                maxima = jnp.max(scores, axis=2, keepdims=True)
                probs = jnp.exp((scores - maxima) * (1.0 / math.sqrt(HD)))
                totals = jnp.sum(probs, axis=2, keepdims=True)
                summed = jnp.dot(
                    probs.reshape(4 * RUN, KEYS).astype(jnp.bfloat16),
                    v_win[:, lanes],
                    preferred_element_type=jnp.float32,
                )
                result = (summed.reshape(4, RUN, HD) / totals).astype(jnp.bfloat16)
                for i in range(4):
                    att_ref[
                        tokens, pl.ds(pl.multiple_of((part * 4 + i) * HD, HD), HD)
                    ] = result[i]
            return inner

        lax.fori_loop(0, QH // 8, eight_heads, 0)
        wide = att_ref[tokens, :].astype(jnp.float32)
        scale = lax.rsqrt(jnp.mean(wide * wide, axis=1, keepdims=True) + norm_eps)
        for cut, (axis, plane, first, width) in enumerate(CUTS):
            span = slice(first, first + width)
            shared[cut][0, tokens, :] = (wide[:, span] * scale * gain_ref[:, span]).astype(
                jnp.bfloat16
            )

    def line_copy(cut, kind, step):
        if kind < 2:
            ref = (all_routes, all_gates)[kind].at[cut]
            source, target = ref.at[0], ref.at[step]
        else:
            run = pl.ds((kind - 2) * RUN, RUN)
            source, target = shared[cut].at[0, run], shared[cut].at[step, run]
        return pltpu.make_async_remote_copy(
            src_ref=source,
            dst_ref=target,
            send_sem=line_send.at[cut, kind, step],
            recv_sem=line_recv.at[cut, kind, step],
            device_id=shift(ctx, exp, line_steps(CUTS[cut][0], step)),
            device_id_type=MESH,
        )

    def share(kinds):
        for kind in kinds:
            for step in (1, 3, 2):
                for cut in range(3):
                    line_copy(cut, kind, step).start()

    for cut in range(3):
        all_routes[cut, 0] = routes_ref[...]
        all_gates[cut, 0] = gates_ref[...]
    attend_run(0)
    pl.semaphore_wait(barrier, 2 * (64 - 27) - 1)
    share((0, 1, 2))
    attend_run(1)
    share((3,))
    for load in loads:
        load.start()

    earlier = ones(
        lax.broadcasted_iota(jnp.int32, (TOK, TOK), 0)
        < lax.broadcasted_iota(jnp.int32, (TOK, TOK), 1)
    )
    def tables(cut, source):
        plane = CUTS[cut][1]
        slot = lax.broadcasted_iota(jnp.int32, (PLANE, TOK), 0)
        at = [jnp.full((PLANE, TOK), 0, jnp.int32) + coordinate for coordinate in place]
        at[plane[0]] = (at[plane[0]] + (slot // 4) % 4) % 4
        at[plane[1]] = (at[plane[1]] + slot % 4) % 4
        ids = (at[0] * 4 + at[1]) * 8 + at[2] * 2 + (core + slot // HALF) % 2
        named = jnp.zeros((PLANE, TOK), jnp.float32)
        weight = jnp.zeros((PLANE, TOK), jnp.float32)
        for k in range(8):
            hit = all_routes[cut, source, k : k + 1, :] == ids
            named = named + hit.astype(jnp.float32)
            weight = weight + jnp.where(hit, all_gates[cut, source, k : k + 1, :], 0.0)
        ranks = jnp.dot(named.astype(jnp.bfloat16), earlier, preferred_element_type=jnp.float32)
        slot_ref[cut, source] = jnp.where(named > 0.5, ranks.astype(jnp.int32), -1)
        weight_ref[cut, source] = weight

    def pack_main(cut, source):
        rows = jnp.dot(
            ones(main_hits(slot_ref[cut, source], PLANE)),
            shared[cut][source],
            preferred_element_type=jnp.float32,
        )
        message[cut][:, source] = rows.astype(jnp.bfloat16).reshape(PLANE, 8, CUTS[cut][3])

    def pack_extra(cut):
        width = CUTS[cut][3]
        hits = jnp.concatenate(
            [ones(extra_hits(slot_ref[cut, source], PLANE, source)) for source in range(4)], axis=1
        )
        rows = jnp.dot(
            hits, shared[cut][...].reshape(4 * TOK, width), preferred_element_type=jnp.float32
        )
        message[cut][:, 4] = rows.astype(jnp.bfloat16).reshape(PLANE, 8, width)

    def sources(cut, first, last, work):
        def one(source, carry):
            work(cut, source)
            return carry

        lax.fori_loop(first, last, one, 0)

    for cut in range(3):
        tables(cut, 0)
        pack_main(cut, 0)
    for cut in range(3):
        for step in (1, 3, 2):
            line_copy(cut, 0, step).wait()
            line_copy(cut, 1, step).wait()
        sources(cut, 1, 4, tables)

    def outward(cut, slot):
        return pltpu.make_async_remote_copy(
            src_ref=message[cut].at[slot],
            dst_ref=arrived[cut].at[slot],
            send_sem=send_out.at[cut, slot],
            recv_sem=recv_out.at[cut, slot],
            device_id=shift(ctx, exp, plane_steps(CUTS[cut][1], slot, 1)),
            device_id_type=MESH,
        )

    def homeward(cut, slot):
        return pltpu.make_async_remote_copy(
            src_ref=message[cut].at[slot],
            dst_ref=returned[cut].at[slot],
            send_sem=send_back.at[cut, slot],
            recv_sem=recv_back.at[cut, slot],
            device_id=shift(ctx, exp, plane_steps(CUTS[cut][1], slot, -1)),
            device_id_type=MESH,
        )

    def own_copy(cut, target, sem):
        return pltpu.make_async_copy(message[cut].at[0], target[cut].at[0], local_sem.at[sem])

    def own_out(cut):
        return own_copy(cut, arrived, 3 + cut)

    def own_back(cut):
        return own_copy(cut, returned, 6 + cut)

    def each(half, cuts, remote, own, begin=0, end=HALF):
        def one(k, carry):
            slot = half * HALF + (k * 7) % HALF

            @pl.when(slot > 0)
            def _():
                for cut in cuts:
                    remote(cut, slot)

            @pl.when(slot == 0)
            def _():
                for cut in cuts:
                    own(cut)

            return carry

        lax.fori_loop(begin, end, one, 0)

    every = (0, 1, 2)
    def send(cut, slot):
        outward(cut, slot).start()

    def send_own(cut):
        own_out(cut).start()

    early = 4
    for step in (1, 3):
        for cut in every:
            line_copy(cut, 2, step).wait()
            line_copy(cut, 3, step).wait()
            pack_main(cut, step)
    for cut in every:
        line_copy(cut, 2, 2).wait()
        line_copy(cut, 3, 2).wait()
        pack_main(cut, 2)
        pack_extra(cut)
        each(0, (cut,), send, send_own, 0, early)
    each(0, every, send, send_own, early, HALF)
    each(1, every, send, send_own)
    for load in loads:
        load.wait()

    def fetch(source, cut, half):
        return pltpu.make_async_copy(
            source[cut].at[pl.ds(half * HALF, HALF)], stage[cut], local_sem.at[9 + cut]
        )

    def expert_half(half, carry):
        for cut in every:
            each(
                half,
                (cut,),
                lambda which, slot: outward(which, slot).wait(),
                lambda which: own_out(which).wait(),
            )
            fetch(arrived, cut, half).start()
        for cut in every:
            fetch(arrived, cut, half).wait()

        def two_z(pair, inner):
            near = pl.ds(pl.multiple_of(pair * 8, 8), 8)
            order_y = extra_order_y()
            order_z = extra_order_z(pair)
            gate = jnp.zeros((320, HID), jnp.float32)
            up = jnp.zeros((320, HID), jnp.float32)
            for cut, (axis, plane, first, width) in enumerate(CUTS):
                if cut == 0:
                    pieces = [
                        stage[0][pl.ds(pair * 8 + k, 1), 0:4].reshape(32, width) for k in range(8)
                    ]
                    pieces.append(stage[0][near, 4].reshape(64, width))
                elif cut == 1:
                    pieces = [
                        stage[1][pl.ds(pair * 8 + z * 4, 4), y].reshape(32, width)
                        for z in range(2)
                        for y in range(4)
                    ]
                    packed = stage[1][near, 4].reshape(64, width)
                    extra = jnp.dot(order_y, packed, preferred_element_type=jnp.float32)
                    pieces.append(extra.astype(jnp.bfloat16))
                else:
                    pieces = [
                        stage[2][:, pair * 2 + z].reshape(128, width) for z in range(2)
                    ]
                    packed = stage[2][:, 4].reshape(128, width)
                    extra = jnp.dot(order_z, packed, preferred_element_type=jnp.float32)
                    pieces.append(extra.astype(jnp.bfloat16))
                rows = jnp.concatenate(pieces, axis=0)
                span = slice(first, first + width)
                gate = gate + jnp.dot(rows, gate_ref[span, :], preferred_element_type=jnp.float32)
                up = up + jnp.dot(rows, up_ref[span, :], preferred_element_type=jnp.float32)
            hidden = (gate / (1.0 + jnp.exp(-gate)) * up).astype(jnp.bfloat16)
            base = half * HALF
            for cut, (axis, plane, first, width) in enumerate(CUTS):
                result = jnp.dot(
                    hidden, down_ref[:, first : first + width], preferred_element_type=jnp.float32
                ).astype(jnp.bfloat16)
                last = result[256:]
                if cut == 0:
                    for k in range(8):
                        message[0][pl.ds(base + pair * 8 + k, 1), 0:4] = result[
                            k * 32 : k * 32 + 32
                        ].reshape(1, 4, 8, width)
                    message[0][pl.ds(base + pair * 8, 8), 4] = last.reshape(8, 8, width)
                elif cut == 1:
                    for z in range(2):
                        for y in range(4):
                            k = z * 4 + y
                            message[1][pl.ds(base + pair * 8 + z * 4, 4), y] = result[
                                k * 32 : k * 32 + 32
                            ].reshape(4, 8, width)
                    spread = lax.dot_general(
                        order_y, last, (((0,), (0,)), ((), ())), preferred_element_type=jnp.float32
                    )
                    message[1][pl.ds(base + pair * 8, 8), 4] = spread.astype(
                        jnp.bfloat16
                    ).reshape(8, 8, width)
                else:
                    whole = pl.ds(base, HALF)
                    for z in range(2):
                        message[2][whole, pair * 2 + z] = result[
                            z * 128 : z * 128 + 128
                        ].reshape(HALF, 8, width)
                    spread = lax.dot_general(
                        order_z, last, (((0,), (0,)), ((), ())), preferred_element_type=jnp.float32
                    ).astype(jnp.bfloat16).reshape(HALF, 8, width)
                    held = message[2][whole, 4]
                    message[2][whole, 4] = spread + jnp.where(
                        pair == 0, jnp.zeros_like(held), held
                    )

            def answer(k, inner):
                slot = base + pair * 8 + (k * 3) % 8
                later = base + ((2 * k) * 7) % HALF
                last = base + ((2 * k + 1) * 7) % HALF

                @pl.when(pair == 1)
                def _():
                    @pl.when(later > 0)
                    def _():
                        homeward(2, later).start()

                    @pl.when(later == 0)
                    def _():
                        own_back(2).start()

                    homeward(2, last).start()

                @pl.when(slot > 0)
                def _():
                    homeward(0, slot).start()
                    homeward(1, slot).start()

                @pl.when(slot == 0)
                def _():
                    own_back(0).start()
                    own_back(1).start()

                return inner

            lax.fori_loop(0, 8, answer, 0)
            return inner

        lax.fori_loop(0, 2, two_z, 0)
        return carry

    lax.fori_loop(0, 2, expert_half, 0)

    def collect_copy(cut, source):
        axis = CUTS[cut][0]
        return pltpu.make_async_remote_copy(
            src_ref=shared[cut].at[source],
            dst_ref=collect[cut].at[source - 1],
            send_sem=line_send.at[cut, 4, source],
            recv_sem=line_recv.at[cut, 4, source],
            device_id=shift(ctx, exp, line_steps(axis, 4 - source)),
            device_id_type=MESH,
        )

    def answers(cut, half, source):
        width = CUTS[cut][3]
        span = pl.ds(half * HALF, HALF)
        slots = slot_ref[cut, source, span, :]
        weights = jnp.broadcast_to(
            weight_ref[cut, source, span, :][:, None, :], (HALF, 8, TOK)
        ).reshape(HALF * 8, TOK)
        value = jnp.concatenate(
            [
                jnp.where(main_hits(slots, HALF), weights, 0.0),
                jnp.where(extra_hits(slots, HALF, source), weights, 0.0),
            ],
            axis=0,
        )
        high = value.astype(jnp.bfloat16)
        low = (value - high.astype(jnp.float32)).astype(jnp.bfloat16)
        factors = jnp.concatenate([high, low], axis=1)
        rows = jnp.concatenate(
            [
                stage[cut][:, source].reshape(HALF * 8, width),
                stage[cut][:, 4].reshape(HALF * 8, width),
            ],
            axis=0,
        )
        both = lax.dot_general(
            factors, rows, (((0,), (0,)), ((), ())), preferred_element_type=jnp.float32
        )
        return both[:TOK] + both[TOK:]

    def columns(cut):
        return slice(CUTS[cut][2], CUTS[cut][2] + CUTS[cut][3])

    def first_sums(cut, source):
        part_sum[source, :, columns(cut)] = answers(cut, 0, source)

    def arrive(cut, half):
        each(half, (cut,), lambda c, slot: homeward(c, slot).wait(), lambda c: own_back(c).wait())
        fetch(returned, cut, half).start()

    def send_sums(cut):
        fetch(returned, cut, 1).wait()

        def one(k, carry):
            source = 1 + (k + 1) % 3
            total = part_sum[source, :, columns(cut)] + answers(cut, 1, source)
            shared[cut][source] = total.astype(jnp.bfloat16)
            collect_copy(cut, source).start()
            return carry

        lax.fori_loop(0, 3, one, 0)

    for cut in every:
        arrive(cut, 0)
    for cut in every:
        fetch(returned, cut, 0).wait()
        sources(cut, 0, 4, first_sums)
    arrive(0, 1)
    arrive(1, 1)
    send_sums(0)
    arrive(2, 1)
    send_sums(1)
    send_sums(2)
    for cut in every:
        part_sum[0, :, columns(cut)] += answers(cut, 1, 0)
    for cut, (axis, plane, first, width) in enumerate(CUTS):
        span = slice(first, first + width)
        total = att_ref[:, span].astype(jnp.float32) + part_sum[0, :, span]
        for source in (1, 3, 2):
            collect_copy(cut, source).wait()
            total = total + collect[cut][source - 1].astype(jnp.float32)
        out_ref[:, span] = total.astype(jnp.bfloat16)


def moe(positions, lengths, queries, keys, values, gain, routes, gates, gate, up, down):
    vmem = pl.BlockSpec(memory_space=pltpu.VMEM)
    hbm = pl.BlockSpec(memory_space=pltpu.HBM)
    widths = [width for axis, plane, first, width in CUTS]
    wire = [(PLANE, 5, 8, width) for width in widths]
    return pl.pallas_call(
        moe_kernel,
        out_shape=[jax.ShapeDtypeStruct((TOK, D), jnp.bfloat16)]
        + [jax.ShapeDtypeStruct(shape, jnp.bfloat16) for shape in wire] * 2,
        in_specs=[pl.BlockSpec(memory_space=pltpu.SMEM)] * 2 + [vmem] * 6 + [hbm] * 3,
        out_specs=[vmem] + [hbm] * 6,
        scratch_shapes=[
            pltpu.VMEM((TOK, D), jnp.bfloat16),
            pltpu.VMEM((KEYS, 256), jnp.bfloat16),
            pltpu.VMEM((KEYS, 256), jnp.bfloat16),
            pltpu.VMEM((D, HID), jnp.bfloat16),
            pltpu.VMEM((D, HID), jnp.bfloat16),
            pltpu.VMEM((HID, D), jnp.bfloat16),
        ]
        + [pltpu.VMEM(shape, jnp.bfloat16) for shape in wire]
        + [pltpu.VMEM((HALF, 5, 8, width), jnp.bfloat16) for width in widths]
        + [pltpu.VMEM((4, TOK, width), jnp.bfloat16) for width in widths]
        + [pltpu.VMEM((3, TOK, width), jnp.bfloat16) for width in widths]
        + [
            pltpu.VMEM((3, 4, 8, TOK), jnp.int32),
            pltpu.VMEM((3, 4, 8, TOK), jnp.float32),
            pltpu.VMEM((3, 4, PLANE, TOK), jnp.int32),
            pltpu.VMEM((3, 4, PLANE, TOK), jnp.float32),
            pltpu.VMEM((4, TOK, D), jnp.float32),
            pltpu.SemaphoreType.DMA((3, 5, 4)),
            pltpu.SemaphoreType.DMA((3, 5, 4)),
            pltpu.SemaphoreType.DMA((3, PLANE)),
            pltpu.SemaphoreType.DMA((3, PLANE)),
            pltpu.SemaphoreType.DMA((3, PLANE)),
            pltpu.SemaphoreType.DMA((3, PLANE)),
            pltpu.SemaphoreType.DMA((12,)),
        ],
        compiler_params=pltpu.CompilerParams(
            collective_id=1, has_side_effects=True, vmem_limit_bytes=62 << 20
        ),
        name="moe",
    )(positions, lengths, queries, keys, values, gain, routes, gates, gate, up, down)[0]


def local(
    query_states,
    key_states,
    value_states,
    positions,
    lengths,
    routes,
    gate_weights,
    norm_gain,
    gate_proj,
    up_proj,
    down_proj,
):
    keys, values = gather_keys(key_states[0], value_states[0])
    out = moe(
        positions,
        lengths,
        query_states[0],
        keys.reshape(BLOCKS, RUN, 256),
        values.reshape(BLOCKS, RUN, 256),
        norm_gain.reshape(1, D),
        routes[0].T,
        gate_weights[0].T,
        gate_proj[0],
        up_proj[0],
        down_proj[0],
    )
    return out[None]


def solution(mesh):
    in_specs = (
        P("exp", "ctx", None),
        P("exp", "ctx", None),
        P("exp", "ctx", None),
        P("exp", None),
        P("exp", None),
        P("exp", "ctx", None),
        P("exp", "ctx", None),
        P(),
        P(("ctx", "exp"), None, None),
        P(("ctx", "exp"), None, None),
        P(("ctx", "exp"), None, None),
    )
    out_specs = P("exp", "ctx", None)
    return jax.shard_map(local, mesh=mesh, in_specs=in_specs, out_specs=out_specs, check_vma=False)
```

```python
import functools
import math

import jax
import jax.numpy as jnp
from jax import lax
from jax.experimental import pallas as pl
from jax.experimental.pallas import tpu as pltpu
from jax.sharding import PartitionSpec as P

QH = 32
HD = 128
D = 4096
HID = 768
TOK = 128
N_CTX = 16
N_DEV = 128
SEQ = 2048
DOCS = 16
RUN = 64
BLOCKS = SEQ // RUN
WINDOW = 10
KEYS = WINDOW * RUN
MESH = pl.DeviceIdType.MESH

neg_large = -1e30
norm_eps = 1e-06


def gather_kernel(k_ref, v_ref, all_k, all_v, send_sem, recv_sem, local_sem):
    out = (all_k, all_v)
    ctx = lax.axis_index("ctx")
    exp = lax.axis_index("exp")

    def along(axis, origin, step):
        oz, oy = origin // 4, origin % 4
        if axis == 0:
            return oz * 4 + (oy + step) % 4
        return ((oz + step) % 4) * 4 + oy

    barrier = pltpu.get_barrier_semaphore()
    for axis in range(2):
        for step in range(1, 4):
            pl.semaphore_signal(
                barrier, inc=1, device_id=(along(axis, ctx, step), exp), device_id_type=MESH
            )
    pl.semaphore_wait(barrier, 6)

    started = []
    for which in range(2):
        for step in range(1, 4):
            sent = pltpu.make_async_remote_copy(
                src_ref=(k_ref, v_ref)[which],
                dst_ref=out[which].at[ctx],
                send_sem=send_sem.at[which, 0, step],
                recv_sem=recv_sem.at[which, 0, step],
                device_id=(along(which, ctx, step), exp),
                device_id_type=MESH,
            )
            sent.start()
            started.append(sent)

    def pass_on(which, first):
        origin = along(which, ctx, 4 - first) if first else ctx
        for step in range(1, 4):
            sent = pltpu.make_async_remote_copy(
                src_ref=out[which].at[origin] if first else (k_ref, v_ref)[which],
                dst_ref=out[which].at[origin],
                send_sem=send_sem.at[which, 1 + first, step],
                recv_sem=recv_sem.at[which, 1 + first, step],
                device_id=(along(1 - which, ctx, step), exp),
                device_id_type=MESH,
            )
            sent.start()
            started.append(sent)

    for which in range(2):
        pass_on(which, 0)
    own = [
        pltpu.make_async_copy(source, out[which].at[ctx], local_sem.at[which])
        for which, source in enumerate((k_ref, v_ref))
    ]
    for sent in own:
        sent.start()
    for first in (1, 3, 2):
        for which in range(2):
            started[which * 3 + first - 1].wait_recv()
            pass_on(which, first)
    for index, sent in enumerate(started):
        sent.wait_send()
        if index >= 6:
            sent.wait_recv()
    for sent in own:
        sent.wait()


def gather_keys(keys, values):
    return pl.pallas_call(
        gather_kernel,
        out_shape=[jax.ShapeDtypeStruct((N_CTX, TOK, 256), jnp.bfloat16)] * 2,
        in_specs=[pl.BlockSpec(memory_space=pltpu.VMEM)] * 2,
        out_specs=[pl.BlockSpec(memory_space=pltpu.VMEM)] * 2,
        scratch_shapes=[
            pltpu.SemaphoreType.DMA((2, 5, 4)),
            pltpu.SemaphoreType.DMA((2, 5, 4)),
            pltpu.SemaphoreType.DMA((2,)),
        ],
        compiler_params=pltpu.CompilerParams(collective_id=0, has_side_effects=True),
        name="gather_keys",
    )(keys, values)


CUTS = ((2, (0, 1), 0, 1536), (1, (0, 2), 1536, 1280), (0, (1, 2), 2816, 1280))
PLANE = 32
HALF = 16


def shift(ctx, exp, steps):
    dz, dy, dx, dcore = steps
    return (
        ((ctx // 4 + dz) % 4) * 4 + (ctx % 4 + dy) % 4,
        ((exp // 2 + dx) % 4) * 2 + (exp % 2 + dcore) % 2,
    )


def line_steps(axis, step):
    steps = [0, 0, 0, 0]
    steps[axis] = step
    return steps


def plane_steps(plane, slot, sign):
    steps = [0, 0, 0, slot // HALF]
    for axis, step in zip(plane, ((slot // 4) % 4, slot % 4)):
        steps[axis] = step if sign > 0 else (4 - step) % 4
    return steps


def ones(hit):
    return hit.astype(jnp.float32).astype(jnp.bfloat16)


def main_hits(slots, count):
    wide = jnp.broadcast_to(slots[:, None, :], (count, 8, TOK))
    return (wide == lax.broadcasted_iota(jnp.int32, (count, 8, TOK), 1)).reshape(count * 8, TOK)


def extra_hits(slots, count, source):
    wide = jnp.broadcast_to(slots[:, None, :], (count, 8, TOK))
    row = lax.broadcasted_iota(jnp.int32, (count, 8, TOK), 1)
    hit = (wide == 8 + row % 2) & (row // 2 == source)
    return hit.reshape(count * 8, TOK)


def extra_order_y():
    row = lax.broadcasted_iota(jnp.int32, (64, 64), 0)
    column = lax.broadcasted_iota(jnp.int32, (64, 64), 1)
    z, y, x, i = row // 32, (row // 8) % 4, (row // 2) % 4, row % 2
    return ones(column == z * 32 + x * 8 + y * 2 + i)


def extra_order_z(half):
    row = lax.broadcasted_iota(jnp.int32, (64, 128), 0)
    column = lax.broadcasted_iota(jnp.int32, (64, 128), 1)
    z, y, x, i = row // 32 + 2 * half, (row // 8) % 4, (row // 2) % 4, row % 2
    return ones(column == (y * 4 + x) * 8 + z * 2 + i)


def moe_kernel(
    pos_ref,
    len_ref,
    q_ref,
    k_ref,
    v_ref,
    gain_ref,
    routes_ref,
    gates_ref,
    gate_hbm,
    up_hbm,
    down_hbm,
    out_ref,
    arrived_0,
    arrived_1,
    arrived_2,
    returned_0,
    returned_1,
    returned_2,
    att_ref,
    k_win,
    v_win,
    gate_ref,
    up_ref,
    down_ref,
    message_0,
    message_1,
    message_2,
    stage_0,
    stage_1,
    stage_2,
    shared_0,
    shared_1,
    shared_2,
    collect_0,
    collect_1,
    collect_2,
    all_routes,
    all_gates,
    slot_ref,
    weight_ref,
    part_sum,
    line_send,
    line_recv,
    send_out,
    recv_out,
    send_back,
    recv_back,
    local_sem,
):
    arrived = (arrived_0, arrived_1, arrived_2)
    returned = (returned_0, returned_1, returned_2)
    message = (message_0, message_1, message_2)
    stage = (stage_0, stage_1, stage_2)
    shared = (shared_0, shared_1, shared_2)
    collect = (collect_0, collect_1, collect_2)
    ctx = lax.axis_index("ctx")
    exp = lax.axis_index("exp")
    place = (ctx // 4, ctx % 4, exp // 2)
    core = exp % 2

    loads = [
        pltpu.make_async_copy(source, target, local_sem.at[i])
        for i, (source, target) in enumerate(
            ((gate_hbm, gate_ref), (up_hbm, up_ref), (down_hbm, down_ref))
        )
    ]

    barrier = pltpu.get_barrier_semaphore()

    def greet(delta, carry):
        dz, dy, dx, dcore = delta // 32, (delta // 8) % 4, (delta // 2) % 4, delta % 2

        @pl.when(dz * dy * dx == 0)
        def _():
            pl.semaphore_signal(
                barrier,
                inc=1,
                device_id=shift(ctx, exp, (dz, dy, dx, dcore)),
                device_id_type=MESH,
            )

        return carry

    lax.fori_loop(1, N_DEV, greet, 0)

    blocks_at = [pos_ref[0, RUN * block] // RUN for block in range(BLOCKS)]
    ends = []
    total = jnp.int32(0)
    for doc in range(DOCS):
        total = total + len_ref[0, doc]
        ends.append(total)

    def attend_run(run):
        first_block = pos_ref[0, ctx * TOK + run * RUN] // RUN

        def window(step, carry):
            wanted = jnp.maximum(first_block - (WINDOW - 1) + step, 0)
            block = jnp.int32(0)
            for index, here in enumerate(blocks_at):
                block = jnp.where(here == wanted, index, block)
            rows = pl.ds(pl.multiple_of(step * RUN, RUN), RUN)
            k_win[rows, :] = k_ref[block]
            v_win[rows, :] = v_ref[block]
            return carry

        lax.fori_loop(0, WINDOW, window, 0)
        own = first_block * RUN + lax.broadcasted_iota(jnp.int32, (RUN, 1), 0)
        start = jnp.zeros((RUN, 1), jnp.int32)
        for end in ends:
            start = jnp.maximum(start, jnp.where(own >= end, end, 0))
        places = (first_block - (WINDOW - 1)) * RUN + lax.broadcasted_iota(
            jnp.int32, (RUN, KEYS), 1
        )
        visible = (places >= start) & (places <= own)
        tokens = slice(run * RUN, run * RUN + RUN)

        def eight_heads(pair, inner):
            chains = []
            for part in (2 * pair, 2 * pair + 1):
                lanes = pl.ds(pl.multiple_of((part // 4) * HD, HD), HD)
                queries = jnp.concatenate(
                    [
                        q_ref[tokens, pl.ds(pl.multiple_of((part * 4 + i) * HD, HD), HD)]
                        for i in range(4)
                    ],
                    axis=0,
                )
                scores = lax.dot_general(
                    queries,
                    k_win[:, lanes],
                    (((1,), (1,)), ((), ())),
                    preferred_element_type=jnp.float32,
                )
                chains.append((part, lanes, scores))
            for part, lanes, scores in chains:
                scores = jnp.where(visible[None], scores.reshape(4, RUN, KEYS), neg_large)
                maxima = jnp.max(scores, axis=2, keepdims=True)
                probs = jnp.exp((scores - maxima) * (1.0 / math.sqrt(HD)))
                totals = jnp.sum(probs, axis=2, keepdims=True)
                summed = jnp.dot(
                    probs.reshape(4 * RUN, KEYS).astype(jnp.bfloat16),
                    v_win[:, lanes],
                    preferred_element_type=jnp.float32,
                )
                result = (summed.reshape(4, RUN, HD) / totals).astype(jnp.bfloat16)
                for i in range(4):
                    att_ref[
                        tokens, pl.ds(pl.multiple_of((part * 4 + i) * HD, HD), HD)
                    ] = result[i]
            return inner

        lax.fori_loop(0, QH // 8, eight_heads, 0)
        wide = att_ref[tokens, :].astype(jnp.float32)
        scale = lax.rsqrt(jnp.mean(wide * wide, axis=1, keepdims=True) + norm_eps)
        for cut, (axis, plane, first, width) in enumerate(CUTS):
            span = slice(first, first + width)
            shared[cut][0, tokens, :] = (wide[:, span] * scale * gain_ref[:, span]).astype(
                jnp.bfloat16
            )

    def line_copy(cut, kind, step):
        if kind < 2:
            ref = (all_routes, all_gates)[kind].at[cut]
            source, target = ref.at[0], ref.at[step]
        else:
            run = pl.ds((kind - 2) * RUN, RUN)
            source, target = shared[cut].at[0, run], shared[cut].at[step, run]
        return pltpu.make_async_remote_copy(
            src_ref=source,
            dst_ref=target,
            send_sem=line_send.at[cut, kind, step],
            recv_sem=line_recv.at[cut, kind, step],
            device_id=shift(ctx, exp, line_steps(CUTS[cut][0], step)),
            device_id_type=MESH,
        )

    def share(kinds):
        for kind in kinds:
            for step in (1, 3, 2):
                for cut in range(3):
                    line_copy(cut, kind, step).start()

    for cut in range(3):
        all_routes[cut, 0] = routes_ref[...]
        all_gates[cut, 0] = gates_ref[...]
    attend_run(0)
    pl.semaphore_wait(barrier, 2 * (64 - 27) - 1)
    share((0, 1, 2))
    attend_run(1)
    share((3,))
    for load in loads:
        load.start()

    earlier = ones(
        lax.broadcasted_iota(jnp.int32, (TOK, TOK), 0)
        < lax.broadcasted_iota(jnp.int32, (TOK, TOK), 1)
    )
    def tables(cut, source):
        plane = CUTS[cut][1]
        slot = lax.broadcasted_iota(jnp.int32, (PLANE, TOK), 0)
        at = [jnp.full((PLANE, TOK), 0, jnp.int32) + coordinate for coordinate in place]
        at[plane[0]] = (at[plane[0]] + (slot // 4) % 4) % 4
        at[plane[1]] = (at[plane[1]] + slot % 4) % 4
        ids = (at[0] * 4 + at[1]) * 8 + at[2] * 2 + (core + slot // HALF) % 2
        named = jnp.zeros((PLANE, TOK), jnp.float32)
        weight = jnp.zeros((PLANE, TOK), jnp.float32)
        for k in range(8):
            hit = all_routes[cut, source, k : k + 1, :] == ids
            named = named + hit.astype(jnp.float32)
            weight = weight + jnp.where(hit, all_gates[cut, source, k : k + 1, :], 0.0)
        ranks = jnp.dot(named.astype(jnp.bfloat16), earlier, preferred_element_type=jnp.float32)
        slot_ref[cut, source] = jnp.where(named > 0.5, ranks.astype(jnp.int32), -1)
        weight_ref[cut, source] = weight

    def pack_main(cut, source):
        rows = jnp.dot(
            ones(main_hits(slot_ref[cut, source], PLANE)),
            shared[cut][source],
            preferred_element_type=jnp.float32,
        )
        message[cut][:, source] = rows.astype(jnp.bfloat16).reshape(PLANE, 8, CUTS[cut][3])

    def pack_extra(cut):
        width = CUTS[cut][3]
        hits = jnp.concatenate(
            [ones(extra_hits(slot_ref[cut, source], PLANE, source)) for source in range(4)], axis=1
        )
        rows = jnp.dot(
            hits, shared[cut][...].reshape(4 * TOK, width), preferred_element_type=jnp.float32
        )
        message[cut][:, 4] = rows.astype(jnp.bfloat16).reshape(PLANE, 8, width)

    def sources(cut, first, last, work):
        def one(source, carry):
            work(cut, source)
            return carry

        lax.fori_loop(first, last, one, 0)

    for cut in range(3):
        tables(cut, 0)
        pack_main(cut, 0)
    for cut in range(3):
        for step in (1, 3, 2):
            line_copy(cut, 0, step).wait()
            line_copy(cut, 1, step).wait()
        sources(cut, 1, 4, tables)

    def outward(cut, slot):
        return pltpu.make_async_remote_copy(
            src_ref=message[cut].at[slot],
            dst_ref=arrived[cut].at[slot],
            send_sem=send_out.at[cut, slot],
            recv_sem=recv_out.at[cut, slot],
            device_id=shift(ctx, exp, plane_steps(CUTS[cut][1], slot, 1)),
            device_id_type=MESH,
        )

    def homeward(cut, slot):
        return pltpu.make_async_remote_copy(
            src_ref=message[cut].at[slot],
            dst_ref=returned[cut].at[slot],
            send_sem=send_back.at[cut, slot],
            recv_sem=recv_back.at[cut, slot],
            device_id=shift(ctx, exp, plane_steps(CUTS[cut][1], slot, -1)),
            device_id_type=MESH,
        )

    def own_copy(cut, target, sem):
        return pltpu.make_async_copy(message[cut].at[0], target[cut].at[0], local_sem.at[sem])

    def own_out(cut):
        return own_copy(cut, arrived, 3 + cut)

    def own_back(cut):
        return own_copy(cut, returned, 6 + cut)

    def each(half, cuts, remote, own, begin=0, end=HALF):
        def one(k, carry):
            slot = half * HALF + (k * 7) % HALF

            @pl.when(slot > 0)
            def _():
                for cut in cuts:
                    remote(cut, slot)

            @pl.when(slot == 0)
            def _():
                for cut in cuts:
                    own(cut)

            return carry

        lax.fori_loop(begin, end, one, 0)

    every = (0, 1, 2)
    def send(cut, slot):
        outward(cut, slot).start()

    def send_own(cut):
        own_out(cut).start()

    early = 4
    for step in (1, 3):
        for cut in every:
            line_copy(cut, 2, step).wait()
            line_copy(cut, 3, step).wait()
            pack_main(cut, step)
    for cut in every:
        line_copy(cut, 2, 2).wait()
        line_copy(cut, 3, 2).wait()
        pack_main(cut, 2)
        pack_extra(cut)
        each(0, (cut,), send, send_own, 0, early)
    each(0, every, send, send_own, early, HALF)
    each(1, every, send, send_own)
    for load in loads:
        load.wait()

    def fetch(source, cut, half):
        return pltpu.make_async_copy(
            source[cut].at[pl.ds(half * HALF, HALF)], stage[cut], local_sem.at[9 + cut]
        )

    def expert_half(half, carry):
        for cut in every:
            each(
                half,
                (cut,),
                lambda which, slot: outward(which, slot).wait(),
                lambda which: own_out(which).wait(),
            )
            fetch(arrived, cut, half).start()
        for cut in every:
            fetch(arrived, cut, half).wait()

        def two_z(pair, inner):
            near = pl.ds(pl.multiple_of(pair * 8, 8), 8)
            order_y = extra_order_y()
            order_z = extra_order_z(pair)
            gate = jnp.zeros((320, HID), jnp.float32)
            up = jnp.zeros((320, HID), jnp.float32)
            for cut, (axis, plane, first, width) in enumerate(CUTS):
                if cut == 0:
                    pieces = [
                        stage[0][pl.ds(pair * 8 + k, 1), 0:4].reshape(32, width) for k in range(8)
                    ]
                    pieces.append(stage[0][near, 4].reshape(64, width))
                elif cut == 1:
                    pieces = [
                        stage[1][pl.ds(pair * 8 + z * 4, 4), y].reshape(32, width)
                        for z in range(2)
                        for y in range(4)
                    ]
                    packed = stage[1][near, 4].reshape(64, width)
                    extra = jnp.dot(order_y, packed, preferred_element_type=jnp.float32)
                    pieces.append(extra.astype(jnp.bfloat16))
                else:
                    pieces = [
                        stage[2][:, pair * 2 + z].reshape(128, width) for z in range(2)
                    ]
                    packed = stage[2][:, 4].reshape(128, width)
                    extra = jnp.dot(order_z, packed, preferred_element_type=jnp.float32)
                    pieces.append(extra.astype(jnp.bfloat16))
                rows = jnp.concatenate(pieces, axis=0)
                span = slice(first, first + width)
                gate = gate + jnp.dot(rows, gate_ref[span, :], preferred_element_type=jnp.float32)
                up = up + jnp.dot(rows, up_ref[span, :], preferred_element_type=jnp.float32)
            hidden = (gate / (1.0 + jnp.exp(-gate)) * up).astype(jnp.bfloat16)
            base = half * HALF
            for cut, (axis, plane, first, width) in enumerate(CUTS):
                result = jnp.dot(
                    hidden, down_ref[:, first : first + width], preferred_element_type=jnp.float32
                ).astype(jnp.bfloat16)
                last = result[256:]
                if cut == 0:
                    for k in range(8):
                        message[0][pl.ds(base + pair * 8 + k, 1), 0:4] = result[
                            k * 32 : k * 32 + 32
                        ].reshape(1, 4, 8, width)
                    message[0][pl.ds(base + pair * 8, 8), 4] = last.reshape(8, 8, width)
                elif cut == 1:
                    for z in range(2):
                        for y in range(4):
                            k = z * 4 + y
                            message[1][pl.ds(base + pair * 8 + z * 4, 4), y] = result[
                                k * 32 : k * 32 + 32
                            ].reshape(4, 8, width)
                    spread = lax.dot_general(
                        order_y, last, (((0,), (0,)), ((), ())), preferred_element_type=jnp.float32
                    )
                    message[1][pl.ds(base + pair * 8, 8), 4] = spread.astype(
                        jnp.bfloat16
                    ).reshape(8, 8, width)
                else:
                    whole = pl.ds(base, HALF)
                    for z in range(2):
                        message[2][whole, pair * 2 + z] = result[
                            z * 128 : z * 128 + 128
                        ].reshape(HALF, 8, width)
                    spread = lax.dot_general(
                        order_z, last, (((0,), (0,)), ((), ())), preferred_element_type=jnp.float32
                    ).astype(jnp.bfloat16).reshape(HALF, 8, width)
                    held = message[2][whole, 4]
                    message[2][whole, 4] = spread + jnp.where(
                        pair == 0, jnp.zeros_like(held), held
                    )

            def answer(k, inner):
                slot = base + pair * 8 + (k * 3) % 8
                later = base + ((2 * k) * 7) % HALF

                @pl.when(pair == 1)
                def _():
                    @pl.when(later > 0)
                    def _():
                        homeward(2, later).start()

                    @pl.when(later == 0)
                    def _():
                        own_back(2).start()

                @pl.when(slot > 0)
                def _():
                    homeward(0, slot).start()
                    homeward(1, slot).start()

                @pl.when(slot == 0)
                def _():
                    own_back(0).start()
                    own_back(1).start()

                return inner

            def answer_last(k, inner):
                homeward(2, base + ((2 * k + 1) * 7) % HALF).start()
                return inner

            lax.fori_loop(0, 8, answer, 0)

            @pl.when(pair == 1)
            def _():
                lax.fori_loop(0, 8, answer_last, 0)

            return inner

        lax.fori_loop(0, 2, two_z, 0)
        return carry

    lax.fori_loop(0, 2, expert_half, 0)

    def collect_copy(cut, source):
        axis = CUTS[cut][0]
        return pltpu.make_async_remote_copy(
            src_ref=shared[cut].at[source],
            dst_ref=collect[cut].at[source - 1],
            send_sem=line_send.at[cut, 4, source],
            recv_sem=line_recv.at[cut, 4, source],
            device_id=shift(ctx, exp, line_steps(axis, 4 - source)),
            device_id_type=MESH,
        )

    def answers(cut, half, source):
        width = CUTS[cut][3]
        span = pl.ds(half * HALF, HALF)
        slots = slot_ref[cut, source, span, :]
        weights = jnp.broadcast_to(
            weight_ref[cut, source, span, :][:, None, :], (HALF, 8, TOK)
        ).reshape(HALF * 8, TOK)
        value = jnp.concatenate(
            [
                jnp.where(main_hits(slots, HALF), weights, 0.0),
                jnp.where(extra_hits(slots, HALF, source), weights, 0.0),
            ],
            axis=0,
        )
        high = value.astype(jnp.bfloat16)
        low = (value - high.astype(jnp.float32)).astype(jnp.bfloat16)
        factors = jnp.concatenate([high, low], axis=1)
        rows = jnp.concatenate(
            [
                stage[cut][:, source].reshape(HALF * 8, width),
                stage[cut][:, 4].reshape(HALF * 8, width),
            ],
            axis=0,
        )
        both = lax.dot_general(
            factors, rows, (((0,), (0,)), ((), ())), preferred_element_type=jnp.float32
        )
        return both[:TOK] + both[TOK:]

    def columns(cut):
        return slice(CUTS[cut][2], CUTS[cut][2] + CUTS[cut][3])

    def first_sums(cut, source):
        part_sum[source, :, columns(cut)] = answers(cut, 0, source)

    def arrive(cut, half):
        each(half, (cut,), lambda c, slot: homeward(c, slot).wait(), lambda c: own_back(c).wait())
        fetch(returned, cut, half).start()

    def send_sums(cut):
        fetch(returned, cut, 1).wait()

        def one(k, carry):
            source = 1 + (k + 1) % 3
            total = part_sum[source, :, columns(cut)] + answers(cut, 1, source)
            shared[cut][source] = total.astype(jnp.bfloat16)
            collect_copy(cut, source).start()
            return carry

        lax.fori_loop(0, 3, one, 0)

    for cut in every:
        arrive(cut, 0)
    for cut in every:
        fetch(returned, cut, 0).wait()
        sources(cut, 0, 4, first_sums)
    arrive(0, 1)
    arrive(1, 1)
    send_sums(0)
    arrive(2, 1)
    send_sums(1)
    send_sums(2)
    for cut in every:
        part_sum[0, :, columns(cut)] += answers(cut, 1, 0)
    for cut, (axis, plane, first, width) in enumerate(CUTS):
        span = slice(first, first + width)
        total = att_ref[:, span].astype(jnp.float32) + part_sum[0, :, span]
        for source in (1, 3, 2):
            collect_copy(cut, source).wait()
            total = total + collect[cut][source - 1].astype(jnp.float32)
        out_ref[:, span] = total.astype(jnp.bfloat16)


def moe(positions, lengths, queries, keys, values, gain, routes, gates, gate, up, down):
    vmem = pl.BlockSpec(memory_space=pltpu.VMEM)
    hbm = pl.BlockSpec(memory_space=pltpu.HBM)
    widths = [width for axis, plane, first, width in CUTS]
    wire = [(PLANE, 5, 8, width) for width in widths]
    return pl.pallas_call(
        moe_kernel,
        out_shape=[jax.ShapeDtypeStruct((TOK, D), jnp.bfloat16)]
        + [jax.ShapeDtypeStruct(shape, jnp.bfloat16) for shape in wire] * 2,
        in_specs=[pl.BlockSpec(memory_space=pltpu.SMEM)] * 2 + [vmem] * 6 + [hbm] * 3,
        out_specs=[vmem] + [hbm] * 6,
        scratch_shapes=[
            pltpu.VMEM((TOK, D), jnp.bfloat16),
            pltpu.VMEM((KEYS, 256), jnp.bfloat16),
            pltpu.VMEM((KEYS, 256), jnp.bfloat16),
            pltpu.VMEM((D, HID), jnp.bfloat16),
            pltpu.VMEM((D, HID), jnp.bfloat16),
            pltpu.VMEM((HID, D), jnp.bfloat16),
        ]
        + [pltpu.VMEM(shape, jnp.bfloat16) for shape in wire]
        + [pltpu.VMEM((HALF, 5, 8, width), jnp.bfloat16) for width in widths]
        + [pltpu.VMEM((4, TOK, width), jnp.bfloat16) for width in widths]
        + [pltpu.VMEM((3, TOK, width), jnp.bfloat16) for width in widths]
        + [
            pltpu.VMEM((3, 4, 8, TOK), jnp.int32),
            pltpu.VMEM((3, 4, 8, TOK), jnp.float32),
            pltpu.VMEM((3, 4, PLANE, TOK), jnp.int32),
            pltpu.VMEM((3, 4, PLANE, TOK), jnp.float32),
            pltpu.VMEM((4, TOK, D), jnp.float32),
            pltpu.SemaphoreType.DMA((3, 5, 4)),
            pltpu.SemaphoreType.DMA((3, 5, 4)),
            pltpu.SemaphoreType.DMA((3, PLANE)),
            pltpu.SemaphoreType.DMA((3, PLANE)),
            pltpu.SemaphoreType.DMA((3, PLANE)),
            pltpu.SemaphoreType.DMA((3, PLANE)),
            pltpu.SemaphoreType.DMA((12,)),
        ],
        compiler_params=pltpu.CompilerParams(
            collective_id=1, has_side_effects=True, vmem_limit_bytes=62 << 20
        ),
        name="moe",
    )(positions, lengths, queries, keys, values, gain, routes, gates, gate, up, down)[0]


def local(
    query_states,
    key_states,
    value_states,
    positions,
    lengths,
    routes,
    gate_weights,
    norm_gain,
    gate_proj,
    up_proj,
    down_proj,
):
    keys, values = gather_keys(key_states[0], value_states[0])
    out = moe(
        positions,
        lengths,
        query_states[0],
        keys.reshape(BLOCKS, RUN, 256),
        values.reshape(BLOCKS, RUN, 256),
        norm_gain.reshape(1, D),
        routes[0].T,
        gate_weights[0].T,
        gate_proj[0],
        up_proj[0],
        down_proj[0],
    )
    return out[None]


def solution(mesh):
    in_specs = (
        P("exp", "ctx", None),
        P("exp", "ctx", None),
        P("exp", "ctx", None),
        P("exp", None),
        P("exp", None),
        P("exp", "ctx", None),
        P("exp", "ctx", None),
        P(),
        P(("ctx", "exp"), None, None),
        P(("ctx", "exp"), None, None),
        P(("ctx", "exp"), None, None),
    )
    out_specs = P("exp", "ctx", None)
    return jax.shard_map(local, mesh=mesh, in_specs=in_specs, out_specs=out_specs, check_vma=False)
```
